32 devices in a mesh: groups: 2 (over x), tm: 8 (over z, y), rows: 2 (over core).
Axes of the slice: x: 2, y: 2, z: 4, core: 2. Of those that a mesh axis runs over, the one named last changes fastest.
Arguments:
- iterate: float32 [32, 512, 512], P(('groups', 'tm'), 'rows'), parts along dimension 0, may hold values from -6 to 6
- forcing: float32 [32, 512, 512], P(('groups', 'tm'), 'rows'), parts along dimension 0, may hold values from -18 to 18
- initial_state: float32 [1024, 512], P(('groups', 'rows')), parts along dimension 0, may hold values from -6 to 6
- diffusivity: float32 [1024, 512], P(('groups', 'rows')), parts along dimension 0, may hold values from 0.5 to 4
Outputs:
- updated: float32 [32, 512, 512], P(('groups', 'tm'), 'rows'), parts along dimension 0
- residual_rms: float32 [32], P(('groups', 'tm')), parts along dimension 0
The draws below stay inside these ranges and needn't reach their ends.
There are 2 independent parts, one for each index of `groups`. The reference program is written for one: setup_inputs(seed, part) draws one part's arguments, and reference() takes and returns one part's arrays. A program takes and returns all parts, laid end to end along the dimension named above; each array names one. Nothing has to cross between parts.
All inputs are finite; a program needn't handle non-finite values.
Results may differ from the reference program's by a relative error of at most 0.0003.
Values sent between devices are 32-bit elements; how exact they have to be, the bound alone decides.
No kernel may reach another device: no remote copies, remote signals or barrier semaphores. Data moves between devices by JAX's collectives and lax.ppermute only.
A program may use at most 64 MiB of HBM per device.

```python
import math
import jax
import jax.numpy as jnp
from jax import lax

NX = 512
NY = 512
CG_ITERS = 3
L = 16


def draw_forcing(key, part):
    dims_all = (L, NX, NY)
    return jax.random.truncated_normal(jax.random.fold_in(key, 17), -6.0, 6.0, dims_all, jnp.float32)


def steps_of(rng, shape, pieces, low, high):
    gain = 1.0
    for dim, parts in pieces:
        draws = jax.random.uniform(jax.random.fold_in(jax.random.fold_in(rng, 6), dim), (parts,), jnp.float32, low / len(pieces), high / len(pieces))
        gain = gain * jnp.repeat(jnp.exp(draws), shape[dim] // parts).reshape((-1,) + (1,) * (len(shape) - 1 - dim))
    return gain


def centred(stream_key, extent, width, reach, shards=(), kind=jnp.bfloat16):
    result = width * jax.random.normal(stream_key, extent, jnp.float32)
    if shards:
        result = result * steps_of(stream_key, extent, shards, -0.22, 0.18)
    return jnp.clip(result, -reach, reach).astype(kind)


def setup_inputs(seed: int = 0, part: int = 0) -> dict:
    streams_of = jax.random.split(jax.random.key(seed), 5)
    own_keys = jax.random.split(jax.random.fold_in(streams_of[4], part), 5)
    iterate = centred(own_keys[0], (L, NX, NY), 1.0, 6.0, ((0, 8), (1, 2)), jnp.float32)
    forcing = draw_forcing(jax.random.fold_in(jax.random.fold_in(streams_of[4], part), 71), part)
    initial_state = centred(own_keys[2], (NX, NY), 1.0, 6.0, ((0, 2),), jnp.float32)
    diffusivity = jnp.clip(jnp.exp(math.log(4.0) - 2.0794415 * jax.random.uniform(own_keys[3], (NX, NY), jnp.float32) ** steps_of(own_keys[3], (NX, NY), ((0, 2),), -0.2, 0.2)), 0.5, 4.0)
    return dict(iterate=iterate, forcing=forcing, initial_state=initial_state, diffusivity=diffusivity)


circulant_alpha = 0.05
time_step = 0.5
rms_eps = 1e-06

def phase_table(first_index, second_index, length):
    product = first_index[:, None] * second_index[None, :] % length
    return 2.0 * jnp.pi / length * product.astype(jnp.float32)

def faces_from(padded_rows):
    centre = padded_rows[1:-1]
    columns = jnp.pad(centre, ((0, 0), (1, 1)), mode='edge')
    north_face = 0.5 * (centre + padded_rows[:-2])
    south_face = 0.5 * (centre + padded_rows[2:])
    west_face = 0.5 * (centre + columns[:, :-2])
    east_face = 0.5 * (centre + columns[:, 2:])
    return (north_face, south_face, west_face, east_face)

def apply_faces(padded_rows, weights):
    north_face, south_face, west_face, east_face = weights
    centre = padded_rows[..., 1:-1, :]
    lead_pad = [(0, 0)] * (centre.ndim - 1)
    columns = jnp.pad(centre, lead_pad + [(1, 1)])
    return (north_face + south_face + west_face + east_face) * centre - north_face * padded_rows[..., :-2, :] - south_face * padded_rows[..., 2:, :] - west_face * columns[..., :-2] - east_face * columns[..., 2:]

def pad_rows(values):
    lead_pad = [(0, 0)] * (values.ndim - 2)
    return jnp.pad(values, lead_pad + [(1, 1), (0, 0)])

def apply_shifted(values, real_shift, imag_shift, weights, orientation):
    spread = time_step * apply_faces(pad_rows(values), weights)
    swapped = jnp.stack([-values[1], values[0]])
    return real_shift * values + orientation * imag_shift * swapped + spread

def normal_solve(rhs_values, real_shift, imag_shift, weights):

    def freq_norm(values):
        return lax.optimization_barrier(jnp.sum(values * values, axis=(0, 2, 3)))

    def expand(values):
        return values[None, :, None, None]
    solution = jnp.zeros_like(rhs_values)
    remain = rhs_values
    normal = apply_shifted(remain, real_shift, imag_shift, weights, -1.0)
    gamma_now = freq_norm(normal)
    search = normal
    for iteration in range(CG_ITERS):
        image_now = apply_shifted(search, real_shift, imag_shift, weights, 1.0)
        step_rate = gamma_now / freq_norm(image_now)
        solution = solution + expand(step_rate) * search
        if iteration + 1 < CG_ITERS:
            remain = remain - expand(step_rate) * image_now
            normal = apply_shifted(remain, real_shift, imag_shift, weights, -1.0)
            gamma_next = freq_norm(normal)
            search = normal + expand(gamma_next / gamma_now) * search
            gamma_now = gamma_next
    return solution

def reference(iterate, forcing, initial_state, diffusivity):
    length = iterate.shape[0]
    cell_count = NX * NY
    faces = faces_from(jnp.pad(diffusivity, ((1, 1), (0, 0)), mode='edge'))
    previous = jnp.concatenate([initial_state[None], iterate[:-1]], axis=0)
    residual = time_step * forcing + previous - iterate - time_step * apply_faces(pad_rows(iterate), faces)
    residual_rms = jnp.sqrt(lax.optimization_barrier(jnp.sum(residual * residual, axis=(1, 2))) / cell_count + rms_eps)
    all_index = jnp.arange(length, dtype=jnp.int32)
    log_alpha = jnp.log(jnp.float32(circulant_alpha))
    growth = jnp.exp(log_alpha * all_index.astype(jnp.float32) / length)
    scaled = residual * growth[:, None, None]
    angles = phase_table(all_index, all_index, length)
    flat_cells = scaled.reshape(length, -1)
    spectrum_real = jnp.dot(jnp.cos(angles), flat_cells, precision=lax.Precision.HIGHEST, preferred_element_type=jnp.float32)
    spectrum_imag = jnp.dot(-jnp.sin(angles), flat_cells, precision=lax.Precision.HIGHEST, preferred_element_type=jnp.float32)
    spectrum = jnp.stack([spectrum_real, spectrum_imag]).reshape(2, length, NX, NY)
    root_alpha = jnp.exp(log_alpha / length)
    freq_angle = 2.0 * jnp.pi / length * all_index.astype(jnp.float32)
    real_shift = (1.0 - root_alpha * jnp.cos(freq_angle))[:, None, None]
    imag_shift = (root_alpha * jnp.sin(freq_angle))[:, None, None]
    solution = normal_solve(spectrum, real_shift, imag_shift, faces)
    flat_real = solution[0].reshape(length, -1)
    flat_imag = solution[1].reshape(length, -1)
    correction = jnp.dot(jnp.cos(angles) / length, flat_real, precision=lax.Precision.HIGHEST, preferred_element_type=jnp.float32) - jnp.dot(jnp.sin(angles) / length, flat_imag, precision=lax.Precision.HIGHEST, preferred_element_type=jnp.float32)
    correction = correction.reshape(length, NX, NY)
    updated = iterate + correction / growth[:, None, None]
    return (updated, residual_rms)
```

```python
import functools
import math

import jax
import jax.numpy as jnp
import numpy as np
from jax import lax
from jax.experimental import pallas as pl
from jax.experimental.pallas import tpu as pltpu
from jax.sharding import PartitionSpec as P

CG_ITERS = 3
DEPTH = 2 * CG_ITERS
MOMENTS = 2 * DEPTH + 1

circulant_alpha = 0.05
time_step = 0.5
rms_eps = 1e-06


def extended(block, sides, width):
    for axis, dim in sides:
        count = lax.axis_size(axis)
        forward = [(i, i + 1) for i in range(count - 1)]
        backward = [(target, source) for source, target in forward]
        low = lax.ppermute(
            lax.slice_in_dim(block, block.shape[dim] - width, None, axis=dim), axis, forward
        )
        high = lax.ppermute(lax.slice_in_dim(block, 0, width, axis=dim), axis, backward)
        block = jnp.concatenate([low, block, high], axis=dim)
    return block


def from_behind(value, axis, steps):
    count = lax.axis_size(axis)
    initial, last = (max(0, -steps), min(count, count - steps))
    return lax.ppermute(value, axis, [(source, source + steps) for source in range(initial, last)])


def faces_from(padded_rows):
    centre = padded_rows[1:-1]
    columns = jnp.pad(centre, ((0, 0), (1, 1)), mode="edge")
    north_face = 0.5 * (centre + padded_rows[:-2])
    south_face = 0.5 * (centre + padded_rows[2:])
    west_face = 0.5 * (centre + columns[:, :-2])
    east_face = 0.5 * (centre + columns[:, 2:])
    return (north_face, south_face, west_face, east_face)


def apply_faces(padded_rows, weights):
    north_face, south_face, west_face, east_face = weights
    centre = padded_rows[..., 1:-1, :]
    lead_pad = [(0, 0)] * (centre.ndim - 1)
    columns = jnp.pad(centre, lead_pad + [(1, 1)])
    return (
        (north_face + south_face + west_face + east_face) * centre
        - north_face * padded_rows[..., :-2, :]
        - south_face * padded_rows[..., 2:, :]
        - west_face * columns[..., :-2]
        - east_face * columns[..., 2:]
    )


def growth_of(length):
    return np.exp(math.log(circulant_alpha) * np.arange(length) / length)


def forward_matrix(length):
    half = length // 2
    steps = np.arange(length)
    table = np.zeros((length, length))
    for j in range(half):
        turn = 2 * np.pi * ((j * steps) % length) / length
        table[j] = np.cos(turn)
        table[half + j] = -np.sin(turn)
    table[half] = np.cos(2 * np.pi * ((half * steps) % length) / length)
    return table * growth_of(length)[None, :]


def inverse_matrix(length):
    half = length // 2
    steps = np.arange(length)
    table = np.zeros((length, length))
    for j in range(half):
        turn = 2 * np.pi * ((j * steps) % length) / length
        weight = 1.0 if j == 0 else 2.0
        table[:, j] = weight * np.cos(turn) / length
        table[:, half + j] = -weight * np.sin(turn) / length
    table[:, half] = np.cos(2 * np.pi * ((half * steps) % length) / length) / length
    return table / growth_of(length)[:, None]


def block_forward(length, rows):
    full = np.einsum("cn,rs->rcns", forward_matrix(length), np.eye(rows))
    return full.reshape(rows * length, length * rows).astype(np.float32)


def block_inverse(length, rows):
    full = np.einsum("nc,rs->nrsc", inverse_matrix(length), np.eye(rows))
    return full.reshape(length * rows, rows * length).astype(np.float32)


def channel_shifts(length):
    half = length // 2
    root = math.exp(math.log(circulant_alpha) / length)
    freq = np.concatenate([np.arange(half), np.arange(half)])
    freq[half] = half
    angle = 2 * np.pi * freq / length
    real = 1 - root * np.cos(angle)
    imag = root * np.sin(angle)
    imag[0] = 0.0
    imag[half] = 0.0
    return real, imag


def power_table(length):
    real, imag = channel_shifts(length)
    base = np.stack([real**2 + imag**2, 2 * real, np.ones_like(real)], axis=1)
    powers = [np.concatenate([np.ones((length, 1)), np.zeros((length, MOMENTS - 1))], axis=1)]
    for _ in range(DEPTH):
        last = powers[-1]
        following = np.zeros_like(last)
        for m in range(3):
            following[:, m:] += base[:, m : m + 1] * last[:, : MOMENTS - m]
        powers.append(following)
    return np.stack(powers)


def krylov_body(length, slab, halo, place_ref, pieces_ref, diff_ref, mix_ref, *rest):
    power_refs = rest[:DEPTH]
    moments_ref = rest[DEPTH]
    vectors = rest[DEPTH + 1 : 2 * DEPTH + 2]
    weights_ref = rest[2 * DEPTH + 2]
    rows = slab + 2 * halo
    columns = diff_ref.shape[-1]
    steps_dev = pieces_ref.shape[1] // rows

    centre = diff_ref[...]
    above = jnp.concatenate([centre[:1], centre[:-1]], axis=0)
    below = jnp.concatenate([centre[1:], centre[-1:]], axis=0)
    lane = lax.broadcasted_iota(jnp.int32, (rows, columns), 1)
    row = lax.broadcasted_iota(jnp.int32, (rows, columns), 0) + place_ref[0]
    left_edge = lane == 0
    right_edge = lane == columns - 1
    before = jnp.where(left_edge, centre, pltpu.roll(centre, 1, 1))
    after = jnp.where(right_edge, centre, pltpu.roll(centre, columns - 1, 1))
    quarter = 0.5 * time_step
    north = quarter * (centre + above)
    south = quarter * (centre + below)
    west = quarter * (centre + before)
    east = quarter * (centre + after)
    weights_ref[0] = north + south + west + east
    weights_ref[1] = jnp.where(row == 0, 0.0, north)
    weights_ref[2] = jnp.where(row == place_ref[1] - 1, 0.0, south)
    weights_ref[3] = jnp.where(left_edge, 0.0, west)
    weights_ref[4] = jnp.where(right_edge, 0.0, east)

    mix = mix_ref[...]
    starts = list(range(0, rows - 7, 8))
    if starts[-1] + 8 < rows:
        starts.append(rows - 8)
    for start in starts:
        cells = []
        for source in range(length // steps_dev):
            for step in range(steps_dev):
                at = step * rows + start
                cells.append(pieces_ref[source, at : at + 8, :])
        block = jnp.concatenate(cells, axis=0)
        vectors[0][start * length : (start + 8) * length, :] = jnp.dot(
            mix, block, precision=lax.Precision.HIGHEST, preferred_element_type=jnp.float32
        )

    def stencil(source, r):
        at = pl.multiple_of(r * length, 8)
        here = source[pl.ds(at, length), :]
        up = source[pl.ds(pl.multiple_of(at - length, 8), length), :]
        down = source[pl.ds(pl.multiple_of(at + length, 8), length), :]

        def weight(index):
            return weights_ref[index, pl.ds(r, 1), :]

        return here, (
            weight(0) * here
            - weight(1) * up
            - weight(2) * down
            - weight(3) * pltpu.roll(here, 1, 1)
            - weight(4) * pltpu.roll(here, columns - 1, 1)
        )

    lanes = lax.broadcasted_iota(jnp.int32, (length, 128), 1)
    table = jnp.zeros((length, 128), jnp.float32)

    def put(table, index, sums):
        return jnp.where(lanes == index, jnp.sum(sums, axis=1, keepdims=True), table)

    for power in range(DEPTH):
        source, target = vectors[power], vectors[power + 1]

        def plain(r, carry):
            _, value = stencil(source, r)
            target[pl.ds(pl.multiple_of(r * length, 8), length), :] = value
            return carry

        def summed(r, carry):
            here, value = stencil(source, r)
            if power + 1 < DEPTH:
                target[pl.ds(pl.multiple_of(r * length, 8), length), :] = value
            squares, products, last = carry
            squares = squares + here * here
            products = products + here * value
            if power + 1 == DEPTH:
                last = last + value * value
            return squares, products, last

        first, final = power + 1, rows - 1 - power
        if first < halo:
            lax.fori_loop(first, halo, plain, 0)
            lax.fori_loop(halo + slab, final, plain, 0)
        zero = jnp.zeros((length, columns), jnp.float32)
        squares, products, last = lax.fori_loop(
            halo, halo + slab, summed, (zero, zero, zero if power + 1 == DEPTH else 0.0)
        )
        table = put(table, 2 * power, squares)
        table = put(table, 2 * power + 1, products)
        if power + 1 == DEPTH:
            table = put(table, 2 * DEPTH, last)
        power_refs[power][...] = source[halo * length : (halo + slab) * length, :]
    moments_ref[...] = table


def combine_body(length, slab, moments_ref, table_ref, shift_ref, mix_ref, *rest):
    power_refs = rest[:DEPTH]
    out_ref = rest[DEPTH]
    steps_dev = out_ref.shape[1] // slab
    half = length // 2
    own = moments_ref[...]
    swapped = jnp.concatenate([own[half:], own[:half]], axis=0)
    channel = lax.broadcasted_iota(jnp.int32, own.shape, 0)
    alone = (channel == 0) | (channel == half)
    sums = jnp.where(alone, own, own + swapped)
    mu = [
        jnp.sum(sums * table_ref[k + 1], axis=1, keepdims=True) for k in range(2 * CG_ITERS)
    ]
    low1, low2 = mu[2] / mu[1], mu[3] / mu[1]
    pivot1 = mu[3] - low1 * mu[2]
    cross = mu[4] - low1 * mu[3]
    pivot2 = mu[5] - low2 * mu[3]
    right1 = mu[1] - low1 * mu[0]
    right2 = mu[2] - low2 * mu[0]
    low3 = cross / pivot1
    pivot2 = pivot2 - low3 * cross
    right2 = right2 - low3 * right1
    c2 = right2 / pivot2
    c1 = (right1 - cross * c2) / pivot1
    c0 = (mu[0] - mu[2] * c1 - mu[3] * c2) / mu[1]
    inner = c0 * table_ref[0] + c1 * table_ref[1] + c2 * table_ref[2]
    real = shift_ref[0]
    imag = shift_ref[1]
    lanes = lax.broadcasted_iota(jnp.int32, inner.shape, 1)
    outer = real * inner + jnp.where(lanes == 0, 0.0, pltpu.roll(inner, 1, 1))
    crossed = imag * inner
    sign = jnp.where(lax.broadcasted_iota(jnp.int32, inner.shape, 0) < half, 1.0, -1.0)
    crossed = sign * crossed
    columns = out_ref.shape[-1]

    def spread(values, index):
        return jnp.broadcast_to(values[:, index : index + 1], (length, columns))[None]

    for start in range(0, slab, 8):
        total = jnp.zeros((8, length, columns), jnp.float32)
        other = jnp.zeros((8, length, columns), jnp.float32)
        for power in range(DEPTH):
            here = power_refs[power][start * length : (start + 8) * length, :].reshape(
                8, length, columns
            )
            total = total + spread(outer, power) * here
            if power + 1 < DEPTH:
                flipped = jnp.concatenate([here[:, half:], here[:, :half]], axis=1)
                other = other + spread(crossed, power) * flipped
        block = (total + other).reshape(8 * length, columns)
        result = jnp.dot(
            mix_ref[...], block, precision=lax.Precision.HIGHEST, preferred_element_type=jnp.float32
        )
        for step in range(length):
            at = (step % steps_dev) * slab + start
            out_ref[step // steps_dev, at : at + 8, :] = result[step * 8 : step * 8 + 8]


def shards(iterate, forcing, initial_state, diffusivity):
    steps_dev, rows_dev, columns_dev = iterate.shape
    time_devices = lax.axis_size("tm")
    row_devices = lax.axis_size("rows")
    time_rank = lax.axis_index("tm")
    row_rank = lax.axis_index("rows")
    length = steps_dev * time_devices
    cell_count = rows_dev * row_devices * columns_dev
    slab = rows_dev // time_devices
    halo = DEPTH
    rows = slab + 2 * halo

    rimmed = extended(diffusivity, (("rows", 0),), halo)
    here = lax.broadcasted_iota(jnp.int32, (rimmed.shape[0], 1), 0)
    rimmed = jnp.where((row_rank == 0) & (here < halo), diffusivity[:1], rimmed)
    rimmed = jnp.where(
        (row_rank == row_devices - 1) & (here >= halo + rows_dev), diffusivity[-1:], rimmed
    )
    local_faces = faces_from(rimmed[halo - 1 : halo + rows_dev + 1])
    arriving = from_behind(iterate[-1], "tm", 1)
    first_previous = jnp.where(time_rank == 0, initial_state, arriving)
    previous = jnp.concatenate([first_previous[None], iterate[:-1]], axis=0)
    iterate_rim = extended(iterate, (("rows", 1),), 1)
    residual = (
        time_step * forcing + previous - iterate - time_step * apply_faces(iterate_rim, local_faces)
    )
    squares = lax.psum(jnp.sum(residual * residual, axis=(1, 2)), "rows")
    residual_rms = jnp.sqrt(squares / cell_count + rms_eps)

    wide = extended(residual, (("rows", 1),), halo)
    pieces = jnp.stack(
        [
            lax.slice_in_dim(wide, slab * k, slab * k + rows, axis=1).reshape(
                steps_dev * rows, columns_dev
            )
            for k in range(time_devices)
        ]
    )
    by_cells = lax.all_to_all(pieces, "tm", split_axis=0, concat_axis=0, tiled=True)
    diff_slab = lax.dynamic_slice_in_dim(rimmed, slab * time_rank, rows, axis=0)
    place = jnp.stack(
        [row_rank * rows_dev + time_rank * slab - halo, jnp.int32(rows_dev * row_devices)]
    ).astype(jnp.int32)

    vmem = pl.BlockSpec(memory_space=pltpu.VMEM)
    smem = pl.BlockSpec(memory_space=pltpu.SMEM)
    own = jax.ShapeDtypeStruct((slab * length, columns_dev), jnp.float32)
    *powers, moments = pl.pallas_call(
        functools.partial(krylov_body, length, slab, halo),
        out_shape=[own] * DEPTH + [jax.ShapeDtypeStruct((length, 128), jnp.float32)],
        in_specs=[smem, vmem, vmem, vmem],
        out_specs=[vmem] * (DEPTH + 1),
        scratch_shapes=[pltpu.VMEM((rows * length, columns_dev), jnp.float32)] * (DEPTH + 1)
        + [pltpu.VMEM((5, rows, columns_dev), jnp.float32)],
        name="krylov",
    )(place, by_cells, diff_slab, jnp.asarray(block_forward(length, 8)))

    for axis in ("rows", "tm"):
        count = lax.axis_size(axis)
        if count & (count - 1):
            moments = lax.psum(moments, axis)
        else:
            step = 1
            while step < count:
                pairs = [(i, i ^ step) for i in range(count)]
                moments = moments + lax.ppermute(moments, axis, pairs)
                step *= 2

    real, imag = channel_shifts(length)
    shift = np.broadcast_to(np.stack([real, imag])[:, :, None], (2, length, 128))
    table = np.zeros((DEPTH + 1, length, 128))
    table[:, :, :MOMENTS] = power_table(length)
    corrected = pl.pallas_call(
        functools.partial(combine_body, length, slab),
        out_shape=jax.ShapeDtypeStruct((time_devices, steps_dev * slab, columns_dev), jnp.float32),
        in_specs=[vmem] * (4 + DEPTH),
        out_specs=vmem,
        name="combine",
    )(
        moments,
        jnp.asarray(table, jnp.float32),
        jnp.asarray(shift, jnp.float32),
        jnp.asarray(block_inverse(length, 8)),
        *powers,
    )
    back = lax.all_to_all(corrected, "tm", split_axis=0, concat_axis=0, tiled=True)
    own_steps = back.reshape(time_devices, steps_dev, slab, columns_dev)
    own_steps = jnp.swapaxes(own_steps, 0, 1).reshape(steps_dev, rows_dev, columns_dev)
    updated = iterate + own_steps
    return (updated, residual_rms)


def solution(mesh):
    placed = (
        P(("groups", "tm"), "rows", None),
        P(("groups", "tm"), "rows", None),
        P(("groups", "rows"), None),
        P(("groups", "rows"), None),
    )
    return jax.shard_map(
        shards,
        mesh=mesh,
        in_specs=placed,
        out_specs=(P(("groups", "tm"), "rows", None), P(("groups", "tm"))),
        check_vma=False,
    )
```

```python
import functools
import math

import jax
import jax.numpy as jnp
import numpy as np
from jax import lax
from jax.experimental import pallas as pl
from jax.experimental.pallas import tpu as pltpu
from jax.sharding import PartitionSpec as P

CG_ITERS = 3
DEPTH = 2 * CG_ITERS
MOMENTS = 2 * DEPTH + 1
UNROLL = 16

circulant_alpha = 0.05
time_step = 0.5
rms_eps = 1e-06


def extended(block, sides, width):
    for axis, dim in sides:
        count = lax.axis_size(axis)
        forward = [(i, i + 1) for i in range(count - 1)]
        backward = [(target, source) for source, target in forward]
        low = lax.ppermute(
            lax.slice_in_dim(block, block.shape[dim] - width, None, axis=dim), axis, forward
        )
        high = lax.ppermute(lax.slice_in_dim(block, 0, width, axis=dim), axis, backward)
        block = jnp.concatenate([low, block, high], axis=dim)
    return block


def from_behind(value, axis, steps):
    count = lax.axis_size(axis)
    initial, last = (max(0, -steps), min(count, count - steps))
    return lax.ppermute(value, axis, [(source, source + steps) for source in range(initial, last)])


def faces_from(padded_rows):
    centre = padded_rows[1:-1]
    columns = jnp.pad(centre, ((0, 0), (1, 1)), mode="edge")
    north_face = 0.5 * (centre + padded_rows[:-2])
    south_face = 0.5 * (centre + padded_rows[2:])
    west_face = 0.5 * (centre + columns[:, :-2])
    east_face = 0.5 * (centre + columns[:, 2:])
    return (north_face, south_face, west_face, east_face)


def apply_faces(padded_rows, weights):
    north_face, south_face, west_face, east_face = weights
    centre = padded_rows[..., 1:-1, :]
    lead_pad = [(0, 0)] * (centre.ndim - 1)
    columns = jnp.pad(centre, lead_pad + [(1, 1)])
    return (
        (north_face + south_face + west_face + east_face) * centre
        - north_face * padded_rows[..., :-2, :]
        - south_face * padded_rows[..., 2:, :]
        - west_face * columns[..., :-2]
        - east_face * columns[..., 2:]
    )


def growth_of(length):
    return np.exp(math.log(circulant_alpha) * np.arange(length) / length)


def forward_matrix(length):
    half = length // 2
    steps = np.arange(length)
    table = np.zeros((length, length))
    for j in range(half):
        turn = 2 * np.pi * ((j * steps) % length) / length
        table[j] = np.cos(turn)
        table[half + j] = -np.sin(turn)
    table[half] = np.cos(2 * np.pi * ((half * steps) % length) / length)
    return table * growth_of(length)[None, :]


def inverse_matrix(length):
    half = length // 2
    steps = np.arange(length)
    table = np.zeros((length, length))
    for j in range(half):
        turn = 2 * np.pi * ((j * steps) % length) / length
        weight = 1.0 if j == 0 else 2.0
        table[:, j] = weight * np.cos(turn) / length
        table[:, half + j] = -weight * np.sin(turn) / length
    table[:, half] = np.cos(2 * np.pi * ((half * steps) % length) / length) / length
    return table / growth_of(length)[:, None]


def block_forward(length, rows):
    full = np.einsum("cn,rs->rcns", forward_matrix(length), np.eye(rows))
    return full.reshape(rows * length, length * rows).astype(np.float32)


def block_inverse(length, rows):
    full = np.einsum("nc,rs->nrsc", inverse_matrix(length), np.eye(rows))
    return full.reshape(length * rows, rows * length).astype(np.float32)


def channel_shifts(length):
    half = length // 2
    root = math.exp(math.log(circulant_alpha) / length)
    freq = np.concatenate([np.arange(half), np.arange(half)])
    freq[half] = half
    angle = 2 * np.pi * freq / length
    real = 1 - root * np.cos(angle)
    imag = root * np.sin(angle)
    imag[0] = 0.0
    imag[half] = 0.0
    return real, imag


def power_table(length):
    real, imag = channel_shifts(length)
    base = np.stack([real**2 + imag**2, 2 * real, np.ones_like(real)], axis=1)
    powers = [np.concatenate([np.ones((length, 1)), np.zeros((length, MOMENTS - 1))], axis=1)]
    for _ in range(DEPTH):
        last = powers[-1]
        following = np.zeros_like(last)
        for m in range(3):
            following[:, m:] += base[:, m : m + 1] * last[:, : MOMENTS - m]
        powers.append(following)
    return np.stack(powers)


def krylov_body(length, slab, halo, place_ref, pieces_ref, diff_ref, mix_ref, *rest):
    vectors = rest[:DEPTH]
    moments_ref, south_ref, east_ref, west_ref = rest[DEPTH:]
    rows = slab + 2 * halo
    columns = diff_ref.shape[-1]
    groups = length // 8
    tiles = columns // 128
    steps_dev = pieces_ref.shape[1] // rows

    centre = diff_ref[...]
    below = jnp.concatenate([centre[1:], centre[-1:]], axis=0)
    lane = lax.broadcasted_iota(jnp.int32, (rows, columns), 1)
    after = jnp.where(lane == columns - 1, centre, pltpu.roll(centre, columns - 1, 1))
    quarter = 0.5 * time_step
    south = quarter * (centre + below)
    east = quarter * (centre + after)
    west = (2.0 * quarter) * centre[:, :128]
    for r in range(rows):
        south_ref[8 * r : 8 * r + 8, :] = jnp.broadcast_to(south[r : r + 1], (8, columns))
        east_ref[8 * r : 8 * r + 8, :] = jnp.broadcast_to(east[r : r + 1], (8, columns))
        west_ref[8 * r : 8 * r + 8, :] = jnp.broadcast_to(west[r : r + 1], (8, 128))
    first_row = place_ref[0] + halo == 0
    last_row = place_ref[0] + halo + slab == place_ref[1]
    keep_above = jnp.where(first_row, 0.0, 1.0)
    keep_below = jnp.where(last_row, 0.0, 1.0)

    mix = mix_ref[...]
    starts = list(range(0, rows - 7, 8))
    if starts[-1] + 8 < rows:
        starts.append(rows - 8)
    for start in starts:
        cells = []
        for source in range(length // steps_dev):
            for step in range(steps_dev):
                at = step * rows + start
                cells.append(pieces_ref[source, at : at + 8, :])
        block = jnp.concatenate(cells, axis=0)
        vectors[0][start * length : (start + 8) * length, :] = jnp.dot(
            mix, block, precision=lax.Precision.HIGHEST, preferred_element_type=jnp.float32
        )

    lane8 = lax.broadcasted_iota(jnp.int32, (8, 128), 1)
    is_first = lane8 == 0
    is_last = lane8 == 127

    def load(source, r, group):
        at = pl.multiple_of(r * length + 8 * group, 8)
        return [source[pl.ds(at, 8), 128 * t : 128 * t + 128] for t in range(tiles)]

    def row_of(ref, r, t):
        return ref[pl.ds(pl.multiple_of(8 * r, 8), 8), 128 * t : 128 * t + 128]

    def south_flux(r, here, under):
        return [row_of(south_ref, r, t) * (under[t] - here[t]) for t in range(tiles)]

    def stencil(r, here, under, north):
        south = south_flux(r, here, under)
        turned = [pltpu.roll(v, 127, 1) for v in here] + [0.0]
        east = [
            row_of(east_ref, r, t) * (jnp.where(is_last, turned[t + 1], turned[t]) - here[t])
            for t in range(tiles)
        ]
        moved = [row_of(west_ref, r, 0) * here[0]] + [pltpu.roll(f, 1, 1) for f in east]
        value = [
            (jnp.where(is_first, moved[t], moved[t + 1]) - east[t]) + (north[t] - south[t])
            for t in range(tiles)
        ]
        return value, south

    def total(parts):
        while len(parts) > 1:
            parts = [parts[i] + parts[i + 1] for i in range(0, len(parts) - 1, 2)] + (
                [parts[-1]] if len(parts) % 2 else []
            )
        return parts[0]

    table = [jnp.zeros((8, 128), jnp.float32) for _ in range(groups)]

    def put(entry, index, sums):
        return jnp.where(lane8 == index, jnp.sum(sums, axis=1, keepdims=True), entry)

    for power in range(DEPTH):
        source = vectors[power]
        target = vectors[power + 1] if power + 1 < DEPTH else None
        first, final = power + 1, rows - 1 - power
        for group in range(groups):

            def step(r, carry, summing):
                here, north, sums = carry
                under = load(source, r + 1, group)
                value, south = stencil(r, here, under, north)
                if target is not None:
                    at = pl.multiple_of(r * length + 8 * group, 8)
                    for t in range(tiles):
                        target[pl.ds(at, 8), 128 * t : 128 * t + 128] = value[t]
                if summing:
                    products = [
                        sums[0] + total([v * v for v in here]),
                        sums[1] + total([v * w for v, w in zip(here, value)]),
                    ]
                    if target is None:
                        products.append(sums[2] + total([w * w for w in value]))
                    sums = tuple(products)
                return tuple(under), tuple(south), sums

            top = load(source, first - 1, group)
            here = load(source, first, group)
            carry = (tuple(here), tuple(south_flux(first - 1, top, here)), ())
            if first < halo:
                carry = lax.fori_loop(
                    first, halo, functools.partial(step, summing=False), carry, unroll=True
                )
            zero = jnp.zeros((8, 128), jnp.float32)
            carry = (carry[0], carry[1], (zero,) * (2 if target is not None else 3))
            carry = lax.fori_loop(
                halo, halo + slab, functools.partial(step, summing=True), carry, unroll=min(UNROLL, max(1, slab // 2))
            )
            for index, sums in enumerate(carry[2]):
                table[group] = put(table[group], 2 * power + index, sums)
            if first < halo:
                carry = (carry[0], carry[1], ())
                lax.fori_loop(
                    halo + slab, final, functools.partial(step, summing=False), carry, unroll=True
                )
            if target is not None and first < halo:
                for r, keep in ((halo - 1, keep_above), (halo + slab, keep_below)):
                    at = r * length + 8 * group
                    target[at : at + 8, :] = target[at : at + 8, :] * keep
    moments_ref[...] = jnp.concatenate(table, axis=0)


def combine_body(length, slab, halo, moments_ref, table_ref, shift_ref, mix_ref, *rest):
    power_refs = rest[:DEPTH]
    out_ref = rest[DEPTH]
    steps_dev = out_ref.shape[1] // slab
    half = length // 2
    own = moments_ref[...]
    swapped = jnp.concatenate([own[half:], own[:half]], axis=0)
    channel = lax.broadcasted_iota(jnp.int32, own.shape, 0)
    alone = (channel == 0) | (channel == half)
    sums = jnp.where(alone, own, own + swapped)
    mu = [
        jnp.sum(sums * table_ref[k + 1], axis=1, keepdims=True) for k in range(2 * CG_ITERS)
    ]
    low1, low2 = mu[2] / mu[1], mu[3] / mu[1]
    pivot1 = mu[3] - low1 * mu[2]
    cross = mu[4] - low1 * mu[3]
    pivot2 = mu[5] - low2 * mu[3]
    right1 = mu[1] - low1 * mu[0]
    right2 = mu[2] - low2 * mu[0]
    low3 = cross / pivot1
    pivot2 = pivot2 - low3 * cross
    right2 = right2 - low3 * right1
    c2 = right2 / pivot2
    c1 = (right1 - cross * c2) / pivot1
    c0 = (mu[0] - mu[2] * c1 - mu[3] * c2) / mu[1]
    inner = c0 * table_ref[0] + c1 * table_ref[1] + c2 * table_ref[2]
    real = shift_ref[0]
    imag = shift_ref[1]
    lanes = lax.broadcasted_iota(jnp.int32, inner.shape, 1)
    outer = real * inner + jnp.where(lanes == 0, 0.0, pltpu.roll(inner, 1, 1))
    crossed = imag * inner
    sign = jnp.where(lax.broadcasted_iota(jnp.int32, inner.shape, 0) < half, 1.0, -1.0)
    crossed = sign * crossed
    columns = out_ref.shape[-1]

    def spread(values, index):
        return jnp.broadcast_to(values[:, index : index + 1], (length, columns))[None]

    for start in range(0, slab, 8):
        total = jnp.zeros((8, length, columns), jnp.float32)
        other = jnp.zeros((8, length, columns), jnp.float32)
        for power in range(DEPTH):
            at = (halo + start) * length
            here = power_refs[power][at : at + 8 * length, :].reshape(8, length, columns)
            total = total + spread(outer, power) * here
            if power + 1 < DEPTH:
                flipped = jnp.concatenate([here[:, half:], here[:, :half]], axis=1)
                other = other + spread(crossed, power) * flipped
        block = (total + other).reshape(8 * length, columns)
        result = jnp.dot(
            mix_ref[...], block, precision=lax.Precision.HIGHEST, preferred_element_type=jnp.float32
        )
        for step in range(length):
            at = (step % steps_dev) * slab + start
            out_ref[step // steps_dev, at : at + 8, :] = result[step * 8 : step * 8 + 8]


def shards(iterate, forcing, initial_state, diffusivity):
    steps_dev, rows_dev, columns_dev = iterate.shape
    time_devices = lax.axis_size("tm")
    row_devices = lax.axis_size("rows")
    time_rank = lax.axis_index("tm")
    row_rank = lax.axis_index("rows")
    length = steps_dev * time_devices
    cell_count = rows_dev * row_devices * columns_dev
    slab = rows_dev // time_devices
    halo = DEPTH
    rows = slab + 2 * halo

    rimmed = extended(diffusivity, (("rows", 0),), halo)
    here = lax.broadcasted_iota(jnp.int32, (rimmed.shape[0], 1), 0)
    rimmed = jnp.where((row_rank == 0) & (here < halo), diffusivity[:1], rimmed)
    rimmed = jnp.where(
        (row_rank == row_devices - 1) & (here >= halo + rows_dev), diffusivity[-1:], rimmed
    )
    local_faces = faces_from(rimmed[halo - 1 : halo + rows_dev + 1])
    arriving = from_behind(iterate[-1], "tm", 1)
    first_previous = jnp.where(time_rank == 0, initial_state, arriving)
    previous = jnp.concatenate([first_previous[None], iterate[:-1]], axis=0)
    iterate_rim = extended(iterate, (("rows", 1),), 1)
    residual = (
        time_step * forcing + previous - iterate - time_step * apply_faces(iterate_rim, local_faces)
    )
    squares = lax.psum(jnp.sum(residual * residual, axis=(1, 2)), "rows")
    residual_rms = jnp.sqrt(squares / cell_count + rms_eps)

    wide = extended(residual, (("rows", 1),), halo)
    pieces = jnp.stack(
        [
            lax.slice_in_dim(wide, slab * k, slab * k + rows, axis=1).reshape(
                steps_dev * rows, columns_dev
            )
            for k in range(time_devices)
        ]
    )
    by_cells = lax.all_to_all(pieces, "tm", split_axis=0, concat_axis=0, tiled=True)
    diff_slab = lax.dynamic_slice_in_dim(rimmed, slab * time_rank, rows, axis=0)
    place = jnp.stack(
        [row_rank * rows_dev + time_rank * slab - halo, jnp.int32(rows_dev * row_devices)]
    ).astype(jnp.int32)

    vmem = pl.BlockSpec(memory_space=pltpu.VMEM)
    smem = pl.BlockSpec(memory_space=pltpu.SMEM)
    vector = pltpu.VMEM((rows * length, columns_dev), jnp.float32)
    *powers, moments = pl.pallas_call(
        functools.partial(krylov_body, length, slab, halo),
        out_shape=[vector] * DEPTH + [jax.ShapeDtypeStruct((length, 128), jnp.float32)],
        in_specs=[smem, vmem, vmem, vmem],
        out_specs=[vmem] * (DEPTH + 1),
        scratch_shapes=[
            pltpu.VMEM((rows * 8, columns_dev), jnp.float32),
            pltpu.VMEM((rows * 8, columns_dev), jnp.float32),
            pltpu.VMEM((rows * 8, 128), jnp.float32),
        ],
        compiler_params=pltpu.CompilerParams(vmem_limit_bytes=24 * 2**20),
        name="krylov",
    )(place, by_cells, diff_slab, jnp.asarray(block_forward(length, 8)))

    for axis in ("rows", "tm"):
        count = lax.axis_size(axis)
        if count & (count - 1):
            moments = lax.psum(moments, axis)
        else:
            step = 1
            while step < count:
                pairs = [(i, i ^ step) for i in range(count)]
                moments = moments + lax.ppermute(moments, axis, pairs)
                step *= 2

    real, imag = channel_shifts(length)
    shift = np.broadcast_to(np.stack([real, imag])[:, :, None], (2, length, 128))
    table = np.zeros((DEPTH + 1, length, 128))
    table[:, :, :MOMENTS] = power_table(length)
    corrected = pl.pallas_call(
        functools.partial(combine_body, length, slab, halo),
        out_shape=jax.ShapeDtypeStruct((time_devices, steps_dev * slab, columns_dev), jnp.float32),
        in_specs=[vmem] * (4 + DEPTH),
        out_specs=vmem,
        compiler_params=pltpu.CompilerParams(vmem_limit_bytes=24 * 2**20),
        name="combine",
    )(
        moments,
        jnp.asarray(table, jnp.float32),
        jnp.asarray(shift, jnp.float32),
        jnp.asarray(block_inverse(length, 8)),
        *powers,
    )
    back = lax.all_to_all(corrected, "tm", split_axis=0, concat_axis=0, tiled=True)
    own_steps = back.reshape(time_devices, steps_dev, slab, columns_dev)
    own_steps = jnp.swapaxes(own_steps, 0, 1).reshape(steps_dev, rows_dev, columns_dev)
    updated = iterate + own_steps
    return (updated, residual_rms)


def solution(mesh):
    placed = (
        P(("groups", "tm"), "rows", None),
        P(("groups", "tm"), "rows", None),
        P(("groups", "rows"), None),
        P(("groups", "rows"), None),
    )
    return jax.shard_map(
        shards,
        mesh=mesh,
        in_specs=placed,
        out_specs=(P(("groups", "tm"), "rows", None), P(("groups", "tm"))),
        check_vma=False,
    )
```

```python
import functools
import math

import jax
import jax.numpy as jnp
import numpy as np
from jax import lax
from jax.experimental import pallas as pl
from jax.experimental.pallas import tpu as pltpu
from jax.sharding import PartitionSpec as P


CG_ITERS = 3
DEPTH = 2 * CG_ITERS
MOMENTS = 2 * DEPTH + 1
UNROLL = 16
PAD = 8

circulant_alpha = 0.05
time_step = 0.5
rms_eps = 1e-06


def from_behind(value, axis, steps):
    count = lax.axis_size(axis)
    initial, last = (max(0, -steps), min(count, count - steps))
    return lax.ppermute(value, axis, [(source, source + steps) for source in range(initial, last)])


def border_rows(blocks, axis, width):
    count = lax.axis_size(axis)
    if count == 2:
        first = lax.axis_index(axis) == 0

        def edge(block):
            return jnp.where(first, block[..., -width:, :], block[..., :width, :])

        mine = jnp.concatenate([edge(block).reshape(-1, block.shape[-1]) for block in blocks])
        got = lax.ppermute(mine, axis, [(0, 1), (1, 0)])
        return got, got
    low = jnp.concatenate([b[..., -width:, :].reshape(-1, b.shape[-1]) for b in blocks])
    high = jnp.concatenate([b[..., :width, :].reshape(-1, b.shape[-1]) for b in blocks])
    return (
        lax.ppermute(low, axis, [(i, i + 1) for i in range(count - 1)]),
        lax.ppermute(high, axis, [(i + 1, i) for i in range(count - 1)]),
    )


def growth_of(length):
    return np.exp(math.log(circulant_alpha) * np.arange(length) / length)


def forward_matrix(length):
    half = length // 2
    steps = np.arange(length)
    table = np.zeros((length, length))
    for j in range(half):
        turn = 2 * np.pi * ((j * steps) % length) / length
        table[j] = np.cos(turn)
        table[half + j] = -np.sin(turn)
    table[half] = np.cos(2 * np.pi * ((half * steps) % length) / length)
    return table * growth_of(length)[None, :]


def inverse_matrix(length):
    half = length // 2
    steps = np.arange(length)
    table = np.zeros((length, length))
    for j in range(half):
        turn = 2 * np.pi * ((j * steps) % length) / length
        weight = 1.0 if j == 0 else 2.0
        table[:, j] = weight * np.cos(turn) / length
        table[:, half + j] = -weight * np.sin(turn) / length
    table[:, half] = np.cos(2 * np.pi * ((half * steps) % length) / length) / length
    return table / growth_of(length)[:, None]


def block_forward(length, rows):
    full = np.einsum("cn,rs->rcns", forward_matrix(length), np.eye(rows))
    return full.reshape(rows * length, length * rows).astype(np.float32)


def block_inverse(length, rows):
    full = np.einsum("nc,rs->nrsc", inverse_matrix(length), np.eye(rows))
    return full.reshape(length * rows, rows * length).astype(np.float32)


def channel_shifts(length):
    half = length // 2
    root = math.exp(math.log(circulant_alpha) / length)
    freq = np.concatenate([np.arange(half), np.arange(half)])
    freq[half] = half
    angle = 2 * np.pi * freq / length
    real = 1 - root * np.cos(angle)
    imag = root * np.sin(angle)
    imag[0] = 0.0
    imag[half] = 0.0
    return real, imag


def power_table(length):
    real, imag = channel_shifts(length)
    base = np.stack([real**2 + imag**2, 2 * real, np.ones_like(real)], axis=1)
    powers = [np.concatenate([np.ones((length, 1)), np.zeros((length, MOMENTS - 1))], axis=1)]
    for _ in range(DEPTH):
        last = powers[-1]
        following = np.zeros_like(last)
        for m in range(3):
            following[:, m:] += base[:, m : m + 1] * last[:, : MOMENTS - m]
        powers.append(following)
    return np.stack(powers)


def flux_terms(here, under_first, east_weight, south_weight, west_weight, north, masks):
    is_first, is_last, is_top, is_bottom = masks
    tiles = len(here)
    south = []
    for t in range(tiles):
        under = jnp.where(
            is_bottom, pltpu.roll(under_first[t], 7, 0), pltpu.roll(here[t], 7, 0)
        )
        south.append(south_weight[t] * (under - here[t]))
    turned = [pltpu.roll(v, 127, 1) for v in here] + [0.0]
    east = [
        east_weight[t] * (jnp.where(is_last, turned[t + 1], turned[t]) - here[t])
        for t in range(tiles)
    ]
    moved = [west_weight * here[0]] + [pltpu.roll(f, 1, 1) for f in east]
    value = []
    for t in range(tiles):
        from_north = jnp.where(is_top, pltpu.roll(north[t], 1, 0), pltpu.roll(south[t], 1, 0))
        value.append(
            (jnp.where(is_first, moved[t], moved[t + 1]) - east[t]) + (from_north - south[t])
        )
    return value, south


def pack(out_ref, at, source_ref, slab, halo):
    rows = slab + 2 * halo
    for target in range(out_ref.shape[0]):
        first = slab * target + PAD - halo
        for t in range(source_ref.shape[-1] // 128):
            out_ref[target, at + rows * t : at + rows * (t + 1), :] = source_ref[
                first : first + rows, 128 * t : 128 * (t + 1)
            ]


def residual_body(slab, halo, rank_ref, iterate_ref, forcing_ref, diff_ref, low_ref, high_ref,
                  pieces_ref, partial_ref, squares_ref, *scratch):
    steps, rows_dev, columns = iterate_ref.shape
    tiles = columns // 128
    blocks = rows_dev // 8 + 2
    lane8 = lax.broadcasted_iota(jnp.int32, (8, 128), 1)
    sub8 = lax.broadcasted_iota(jnp.int32, (8, 128), 0)
    masks = (lane8 == 0, lane8 == 127, sub8 == 0, sub8 == 7)
    is_low_edge = rank_ref[0] == 0
    is_high_edge = rank_ref[0] == rank_ref[1] - 1
    keep_low = jnp.where(is_low_edge, 0.0, 1.0)
    keep_high = jnp.where(is_high_edge, 0.0, 1.0)

    def cut(ref, at, lead=()):
        return [ref[lead + (slice(at, at + 8), slice(128 * t, 128 * t + 128))] for t in range(tiles)]

    def block_of(ref, step, slot, b):
        if b == 0:
            return [v * keep_low for v in cut(low_ref, 8 * slot)]
        if b == blocks - 1:
            return [v * keep_high for v in cut(high_ref, 8 * slot)]
        return cut(ref, 8 * (b - 1), (step,))

    def diff_of(b):
        if b == 0:
            mine = [
                jnp.broadcast_to(diff_ref[0:1, 128 * t : 128 * t + 128], (8, 128))
                for t in range(tiles)
            ]
            got = cut(low_ref, 16 * steps)
            return [jnp.where(is_low_edge, m, g) for m, g in zip(mine, got)]
        if b == blocks - 1:
            mine = [
                jnp.broadcast_to(diff_ref[rows_dev - 1 :, 128 * t : 128 * t + 128], (8, 128))
                for t in range(tiles)
            ]
            got = cut(high_ref, 16 * steps)
            return [jnp.where(is_high_edge, m, g) for m, g in zip(mine, got)]
        return cut(diff_ref, 8 * (b - 1))

    quarter = 0.5 * time_step
    zeros = [jnp.zeros((8, 128), jnp.float32)] * tiles
    diff = diff_of(0)
    here = [block_of(iterate_ref, s, s, 0) for s in range(steps)]
    north = [zeros] * steps
    squares = [jnp.zeros((8, 128), jnp.float32)] * steps
    for b in range(blocks):
        last = b + 1 == blocks
        diff_next = diff if last else diff_of(b + 1)
        next_here = here if last else [block_of(iterate_ref, s, s, b + 1) for s in range(steps)]
        below = [
            jnp.where(masks[3], pltpu.roll(diff_next[t], 7, 0), pltpu.roll(diff[t], 7, 0))
            for t in range(tiles)
        ]
        turned = [pltpu.roll(v, 127, 1) for v in diff] + [diff[-1]]
        after = [jnp.where(masks[1], turned[t + 1], turned[t]) for t in range(tiles)]
        south_weight = [quarter * (diff[t] + below[t]) for t in range(tiles)]
        east_weight = [quarter * (diff[t] + after[t]) for t in range(tiles)]
        west_weight = (2.0 * quarter) * diff[0]
        for s in range(steps):
            value, north[s] = flux_terms(
                here[s], next_here[s], east_weight, south_weight, west_weight, north[s], masks
            )
            force = block_of(forcing_ref, s, steps + s, b)
            for t in range(tiles):
                left = time_step * force[t] - here[s][t] - value[t]
                if b == 0:
                    left = left * keep_low
                elif last:
                    left = left * keep_high
                if s == 0:
                    partial_ref[8 * b : 8 * b + 8, 128 * t : 128 * t + 128] = left
                else:
                    left = left + here[s - 1][t]
                    scratch[s - 1][8 * b : 8 * b + 8, 128 * t : 128 * t + 128] = left
                    if 0 < b < blocks - 1:
                        squares[s] = squares[s] + left * left
        diff, here = diff_next, next_here
    for s in range(1, steps):
        squares_ref[s - 1] = squares[s]
        pack(pieces_ref, (s - 1) * tiles * (slab + 2 * halo), scratch[s - 1], slab, halo)


def first_step_body(slab, halo, rank_ref, partial_ref, previous_ref, low_ref, high_ref,
                    pieces_ref, squares_ref, whole_ref):
    rows_dev, columns = previous_ref.shape
    keep_low = jnp.where(rank_ref[0] == 0, 0.0, 1.0)
    keep_high = jnp.where(rank_ref[0] == rank_ref[1] - 1, 0.0, 1.0)
    whole_ref[:PAD, :] = partial_ref[:PAD, :] + keep_low * low_ref[...]
    whole_ref[PAD + rows_dev :, :] = partial_ref[PAD + rows_dev :, :] + keep_high * high_ref[...]
    squares = jnp.zeros((8, columns), jnp.float32)
    for at in range(0, rows_dev, 8):
        value = partial_ref[PAD + at : PAD + at + 8, :] + previous_ref[at : at + 8, :]
        whole_ref[PAD + at : PAD + at + 8, :] = value
        squares = squares + value * value
    total = squares[:, :128]
    for t in range(1, columns // 128):
        total = total + squares[:, 128 * t : 128 * t + 128]
    squares_ref[0] = total
    pack(pieces_ref, 0, whole_ref, slab, halo)


def krylov_body(length, slab, halo, place_ref, early_ref, late_ref, diff_ref, mix_ref, *rest):
    vectors = rest[:DEPTH]
    moments_ref, south_ref, east_ref, west_ref = rest[DEPTH:]
    rows = slab + 2 * halo
    columns = diff_ref.shape[-1]
    groups = length // 8
    tiles = columns // 128
    steps_dev = early_ref.shape[1] // (rows * tiles) + 1

    centre = diff_ref[...]
    below = jnp.concatenate([centre[1:], centre[-1:]], axis=0)
    lane = lax.broadcasted_iota(jnp.int32, (rows, columns), 1)
    after = jnp.where(lane == columns - 1, centre, pltpu.roll(centre, columns - 1, 1))
    quarter = 0.5 * time_step
    south = quarter * (centre + below)
    east = quarter * (centre + after)
    west = (2.0 * quarter) * centre[:, :128]
    for r in range(rows):
        south_ref[8 * r : 8 * r + 8, :] = jnp.broadcast_to(south[r : r + 1], (8, columns))
        east_ref[8 * r : 8 * r + 8, :] = jnp.broadcast_to(east[r : r + 1], (8, columns))
        west_ref[8 * r : 8 * r + 8, :] = jnp.broadcast_to(west[r : r + 1], (8, 128))
    first_row = place_ref[0] + halo == 0
    last_row = place_ref[0] + halo + slab == place_ref[1]
    keep_above = jnp.where(first_row, 0.0, 1.0)
    keep_below = jnp.where(last_row, 0.0, 1.0)

    mix = mix_ref[...]
    starts = list(range(0, rows - 7, 8))
    if starts[-1] + 8 < rows:
        starts.append(rows - 8)
    for start in starts:
        for t in range(tiles):
            cells = []
            for source in range(length // steps_dev):
                for step in range(steps_dev):
                    ref = late_ref if step == 0 else early_ref
                    at = (max(step - 1, 0) * tiles + t) * rows + start
                    cells.append(ref[source, at : at + 8, :])
            vectors[0][start * length : (start + 8) * length, 128 * t : 128 * t + 128] = jnp.dot(
                mix,
                jnp.concatenate(cells, axis=0),
                precision=lax.Precision.HIGHEST,
                preferred_element_type=jnp.float32,
            )

    lane8 = lax.broadcasted_iota(jnp.int32, (8, 128), 1)
    is_first = lane8 == 0
    is_last = lane8 == 127

    def load(source, r, group):
        at = pl.multiple_of(r * length + 8 * group, 8)
        return [source[pl.ds(at, 8), 128 * t : 128 * t + 128] for t in range(tiles)]

    def row_of(ref, r, t):
        return ref[pl.ds(pl.multiple_of(8 * r, 8), 8), 128 * t : 128 * t + 128]

    def south_flux(r, here, under):
        return [row_of(south_ref, r, t) * (under[t] - here[t]) for t in range(tiles)]

    def stencil(r, here, under, north):
        south = south_flux(r, here, under)
        turned = [pltpu.roll(v, 127, 1) for v in here] + [0.0]
        east = [
            row_of(east_ref, r, t) * (jnp.where(is_last, turned[t + 1], turned[t]) - here[t])
            for t in range(tiles)
        ]
        moved = [row_of(west_ref, r, 0) * here[0]] + [pltpu.roll(f, 1, 1) for f in east]
        value = [
            (jnp.where(is_first, moved[t], moved[t + 1]) - east[t]) + (north[t] - south[t])
            for t in range(tiles)
        ]
        return value, south

    def total(parts):
        while len(parts) > 1:
            parts = [parts[i] + parts[i + 1] for i in range(0, len(parts) - 1, 2)] + (
                [parts[-1]] if len(parts) % 2 else []
            )
        return parts[0]

    table = [jnp.zeros((8, 128), jnp.float32) for _ in range(groups)]

    def put(entry, index, sums):
        return jnp.where(lane8 == index, jnp.sum(sums, axis=1, keepdims=True), entry)

    for power in range(DEPTH):
        source = vectors[power]
        target = vectors[power + 1] if power + 1 < DEPTH else None
        first, final = power + 1, rows - 1 - power
        for group in range(groups):

            def step(r, carry, summing):
                here, north, sums = carry
                under = load(source, r + 1, group)
                value, south = stencil(r, here, under, north)
                if target is not None:
                    at = pl.multiple_of(r * length + 8 * group, 8)
                    for t in range(tiles):
                        target[pl.ds(at, 8), 128 * t : 128 * t + 128] = value[t]
                if summing:
                    products = [
                        sums[0] + total([v * v for v in here]),
                        sums[1] + total([v * w for v, w in zip(here, value)]),
                    ]
                    if target is None:
                        products.append(sums[2] + total([w * w for w in value]))
                    sums = tuple(products)
                return tuple(under), tuple(south), sums

            top = load(source, first - 1, group)
            here = load(source, first, group)
            carry = (tuple(here), tuple(south_flux(first - 1, top, here)), ())
            if first < halo:
                carry = lax.fori_loop(
                    first, halo, functools.partial(step, summing=False), carry, unroll=True
                )
            zero = jnp.zeros((8, 128), jnp.float32)
            carry = (carry[0], carry[1], (zero,) * (2 if target is not None else 3))
            carry = lax.fori_loop(
                halo, halo + slab, functools.partial(step, summing=True), carry, unroll=min(UNROLL, max(1, slab // 2))
            )
            for index, sums in enumerate(carry[2]):
                table[group] = put(table[group], 2 * power + index, sums)
            if first < halo:
                carry = (carry[0], carry[1], ())
                lax.fori_loop(
                    halo + slab, final, functools.partial(step, summing=False), carry, unroll=True
                )
            if target is not None and first < halo:
                for r, keep in ((halo - 1, keep_above), (halo + slab, keep_below)):
                    at = r * length + 8 * group
                    target[at : at + 8, :] = target[at : at + 8, :] * keep
    moments_ref[...] = jnp.concatenate(table, axis=0)


def combine_body(length, slab, halo, moments_ref, table_ref, shift_ref, mix_ref, *rest):
    power_refs = rest[:DEPTH]
    out_ref = rest[DEPTH]
    steps_dev = out_ref.shape[1] // slab
    half = length // 2
    own = moments_ref[...]
    swapped = jnp.concatenate([own[half:], own[:half]], axis=0)
    channel = lax.broadcasted_iota(jnp.int32, own.shape, 0)
    alone = (channel == 0) | (channel == half)
    sums = jnp.where(alone, own, own + swapped)
    mu = [
        jnp.sum(sums * table_ref[k + 1], axis=1, keepdims=True) for k in range(2 * CG_ITERS)
    ]
    low1, low2 = mu[2] / mu[1], mu[3] / mu[1]
    pivot1 = mu[3] - low1 * mu[2]
    cross = mu[4] - low1 * mu[3]
    pivot2 = mu[5] - low2 * mu[3]
    right1 = mu[1] - low1 * mu[0]
    right2 = mu[2] - low2 * mu[0]
    low3 = cross / pivot1
    pivot2 = pivot2 - low3 * cross
    right2 = right2 - low3 * right1
    c2 = right2 / pivot2
    c1 = (right1 - cross * c2) / pivot1
    c0 = (mu[0] - mu[2] * c1 - mu[3] * c2) / mu[1]
    inner = c0 * table_ref[0] + c1 * table_ref[1] + c2 * table_ref[2]
    real = shift_ref[0]
    imag = shift_ref[1]
    lanes = lax.broadcasted_iota(jnp.int32, inner.shape, 1)
    outer = real * inner + jnp.where(lanes == 0, 0.0, pltpu.roll(inner, 1, 1))
    crossed = imag * inner
    sign = jnp.where(lax.broadcasted_iota(jnp.int32, inner.shape, 0) < half, 1.0, -1.0)
    crossed = sign * crossed
    columns = out_ref.shape[-1]

    def spread(values, index):
        return jnp.broadcast_to(values[:, index : index + 1], (length, columns))[None]

    for start in range(0, slab, 8):
        total = jnp.zeros((8, length, columns), jnp.float32)
        other = jnp.zeros((8, length, columns), jnp.float32)
        for power in range(DEPTH):
            at = (halo + start) * length
            here = power_refs[power][at : at + 8 * length, :].reshape(8, length, columns)
            total = total + spread(outer, power) * here
            if power + 1 < DEPTH:
                flipped = jnp.concatenate([here[:, half:], here[:, :half]], axis=1)
                other = other + spread(crossed, power) * flipped
        block = (total + other).reshape(8 * length, columns)
        result = jnp.dot(
            mix_ref[...], block, precision=lax.Precision.HIGHEST, preferred_element_type=jnp.float32
        )
        for step in range(length):
            at = (step % steps_dev) * slab + start
            out_ref[step // steps_dev, at : at + 8, :] = result[step * 8 : step * 8 + 8]


def iteration(iterate, forcing, initial_state, diffusivity):
    steps_dev, rows_dev, columns_dev = iterate.shape
    time_devices = lax.axis_size("tm")
    row_devices = lax.axis_size("rows")
    time_rank = lax.axis_index("tm")
    row_rank = lax.axis_index("rows")
    length = steps_dev * time_devices
    cell_count = rows_dev * row_devices * columns_dev
    slab = rows_dev // time_devices
    halo = DEPTH
    rows = slab + 2 * halo

    tiles = columns_dev // 128
    vmem = pl.BlockSpec(memory_space=pltpu.VMEM)
    smem = pl.BlockSpec(memory_space=pltpu.SMEM)
    params = pltpu.CompilerParams(vmem_limit_bytes=24 * 2**20)
    rank = jnp.stack([row_rank, jnp.int32(row_devices)]).astype(jnp.int32)

    arriving = from_behind(iterate[-1], "tm", 1)
    low, high = border_rows((iterate, forcing, diffusivity), "rows", PAD)
    padded = rows_dev + 2 * PAD
    early, partial, squares_late = pl.pallas_call(
        functools.partial(residual_body, slab, halo),
        out_shape=[
            jax.ShapeDtypeStruct(
                (time_devices, (steps_dev - 1) * tiles * rows, 128), jnp.float32
            ),
            pltpu.VMEM((padded, columns_dev), jnp.float32),
            jax.ShapeDtypeStruct((steps_dev - 1, 8, 128), jnp.float32),
        ],
        in_specs=[smem] + [vmem] * 5,
        out_specs=[vmem] * 3,
        scratch_shapes=[pltpu.VMEM((padded, columns_dev), jnp.float32)] * (steps_dev - 1),
        compiler_params=params,
        name="residual",
    )(rank, iterate, forcing, diffusivity, low, high)
    early = lax.all_to_all(early, "tm", split_axis=0, concat_axis=0, tiled=True)

    previous = jnp.where(time_rank == 0, initial_state, arriving)
    before_low, before_high = border_rows((previous,), "rows", PAD)
    late, squares_first = pl.pallas_call(
        functools.partial(first_step_body, slab, halo),
        out_shape=[
            jax.ShapeDtypeStruct((time_devices, tiles * rows, 128), jnp.float32),
            jax.ShapeDtypeStruct((1, 8, 128), jnp.float32),
        ],
        in_specs=[smem] + [vmem] * 4,
        out_specs=[vmem] * 2,
        scratch_shapes=[pltpu.VMEM((padded, columns_dev), jnp.float32)],
        compiler_params=params,
        name="first_step",
    )(rank, partial, previous, before_low, before_high)
    late = lax.all_to_all(late, "tm", split_axis=0, concat_axis=0, tiled=True)

    squares = jnp.sum(jnp.concatenate([squares_first, squares_late]), axis=(1, 2))
    residual_rms = jnp.sqrt(lax.psum(squares, "rows") / cell_count + rms_eps)

    diff_low = jnp.where(row_rank == 0, diffusivity[:1], low[-PAD:])
    diff_high = jnp.where(row_rank == row_devices - 1, diffusivity[-1:], high[-PAD:])
    rimmed = jnp.concatenate([diff_low, diffusivity, diff_high])
    diff_slab = lax.dynamic_slice_in_dim(rimmed, slab * time_rank + PAD - halo, rows, axis=0)
    place = jnp.stack(
        [row_rank * rows_dev + time_rank * slab - halo, jnp.int32(rows_dev * row_devices)]
    ).astype(jnp.int32)

    vector = pltpu.VMEM((rows * length, columns_dev), jnp.float32)
    *powers, moments = pl.pallas_call(
        functools.partial(krylov_body, length, slab, halo),
        out_shape=[vector] * DEPTH + [jax.ShapeDtypeStruct((length, 128), jnp.float32)],
        in_specs=[smem] + [vmem] * 4,
        out_specs=[vmem] * (DEPTH + 1),
        scratch_shapes=[
            pltpu.VMEM((rows * 8, columns_dev), jnp.float32),
            pltpu.VMEM((rows * 8, columns_dev), jnp.float32),
            pltpu.VMEM((rows * 8, 128), jnp.float32),
        ],
        compiler_params=params,
        name="krylov",
    )(place, early, late, diff_slab, jnp.asarray(block_forward(length, 8)))

    for axis in ("rows", "tm"):
        count = lax.axis_size(axis)
        if count & (count - 1):
            moments = lax.psum(moments, axis)
        else:
            step = 1
            while step < count:
                pairs = [(i, i ^ step) for i in range(count)]
                moments = moments + lax.ppermute(moments, axis, pairs)
                step *= 2

    real, imag = channel_shifts(length)
    shift = np.broadcast_to(np.stack([real, imag])[:, :, None], (2, length, 128))
    table = np.zeros((DEPTH + 1, length, 128))
    table[:, :, :MOMENTS] = power_table(length)
    corrected = pl.pallas_call(
        functools.partial(combine_body, length, slab, halo),
        out_shape=jax.ShapeDtypeStruct((time_devices, steps_dev * slab, columns_dev), jnp.float32),
        in_specs=[vmem] * (4 + DEPTH),
        out_specs=vmem,
        compiler_params=params,
        name="combine",
    )(
        moments,
        jnp.asarray(table, jnp.float32),
        jnp.asarray(shift, jnp.float32),
        jnp.asarray(block_inverse(length, 8)),
        *powers,
    )
    back = lax.all_to_all(corrected, "tm", split_axis=0, concat_axis=0, tiled=True)
    own_steps = back.reshape(time_devices, steps_dev, slab, columns_dev)
    own_steps = jnp.swapaxes(own_steps, 0, 1).reshape(steps_dev, rows_dev, columns_dev)
    updated = iterate + own_steps
    return (updated, residual_rms)


def solution(mesh):
    placed = (
        P(("groups", "tm"), "rows", None),
        P(("groups", "tm"), "rows", None),
        P(("groups", "rows"), None),
        P(("groups", "rows"), None),
    )
    return jax.shard_map(
        iteration,
        mesh=mesh,
        in_specs=placed,
        out_specs=(P(("groups", "tm"), "rows", None), P(("groups", "tm"))),
        check_vma=False,
    )
```

```python
import functools
import math

import jax
import jax.numpy as jnp
import numpy as np
from jax import lax
from jax.experimental import pallas as pl
from jax.experimental.pallas import tpu as pltpu
from jax.sharding import PartitionSpec as P


CG_ITERS = 3
DEPTH = 2 * CG_ITERS
MOMENTS = 2 * DEPTH + 1
UNROLL = 16
PAD = 8

circulant_alpha = 0.05
time_step = 0.5
rms_eps = 1e-06


def from_behind(value, axis, steps):
    count = lax.axis_size(axis)
    initial, last = (max(0, -steps), min(count, count - steps))
    return lax.ppermute(value, axis, [(source, source + steps) for source in range(initial, last)])


def exchanged(pieces):
    count = pieces.shape[0]
    got = [pieces[0]] + [None] * (count - 1)
    for k in reversed(range(1, count)):
        got[k] = lax.ppermute(pieces[k], "tm", [(i, i ^ k) for i in range(count)])
    return got


def border_rows(blocks, axis, width):
    count = lax.axis_size(axis)
    if count == 2:
        first = lax.axis_index(axis) == 0

        def edge(block):
            return jnp.where(first, block[..., -width:, :], block[..., :width, :])

        mine = jnp.concatenate([edge(block).reshape(-1, block.shape[-1]) for block in blocks])
        got = lax.ppermute(mine, axis, [(0, 1), (1, 0)])
        return got, got
    low = jnp.concatenate([b[..., -width:, :].reshape(-1, b.shape[-1]) for b in blocks])
    high = jnp.concatenate([b[..., :width, :].reshape(-1, b.shape[-1]) for b in blocks])
    return (
        lax.ppermute(low, axis, [(i, i + 1) for i in range(count - 1)]),
        lax.ppermute(high, axis, [(i + 1, i) for i in range(count - 1)]),
    )


def growth_of(length):
    return np.exp(math.log(circulant_alpha) * np.arange(length) / length)


def forward_matrix(length):
    half = length // 2
    steps = np.arange(length)
    table = np.zeros((length, length))
    for j in range(half):
        turn = 2 * np.pi * ((j * steps) % length) / length
        table[j] = np.cos(turn)
        table[half + j] = -np.sin(turn)
    table[half] = np.cos(2 * np.pi * ((half * steps) % length) / length)
    return table * growth_of(length)[None, :]


def inverse_matrix(length):
    half = length // 2
    steps = np.arange(length)
    table = np.zeros((length, length))
    for j in range(half):
        turn = 2 * np.pi * ((j * steps) % length) / length
        weight = 1.0 if j == 0 else 2.0
        table[:, j] = weight * np.cos(turn) / length
        table[:, half + j] = -weight * np.sin(turn) / length
    table[:, half] = np.cos(2 * np.pi * ((half * steps) % length) / length) / length
    return table / growth_of(length)[:, None]


def block_forward(length, rows):
    full = np.einsum("cn,rs->rcns", forward_matrix(length), np.eye(rows))
    return full.reshape(rows * length, length * rows).astype(np.float32)


def block_inverse(length, rows):
    full = np.einsum("nc,rs->nrsc", inverse_matrix(length), np.eye(rows))
    return full.reshape(length * rows, rows * length).astype(np.float32)


def channel_shifts(length):
    half = length // 2
    root = math.exp(math.log(circulant_alpha) / length)
    freq = np.concatenate([np.arange(half), np.arange(half)])
    freq[half] = half
    angle = 2 * np.pi * freq / length
    real = 1 - root * np.cos(angle)
    imag = root * np.sin(angle)
    imag[0] = 0.0
    imag[half] = 0.0
    return real, imag


def power_table(length):
    real, imag = channel_shifts(length)
    base = np.stack([real**2 + imag**2, 2 * real, np.ones_like(real)], axis=1)
    powers = [np.concatenate([np.ones((length, 1)), np.zeros((length, MOMENTS - 1))], axis=1)]
    for _ in range(DEPTH):
        last = powers[-1]
        following = np.zeros_like(last)
        for m in range(3):
            following[:, m:] += base[:, m : m + 1] * last[:, : MOMENTS - m]
        powers.append(following)
    return np.stack(powers)


def face_weights(padded_rows):
    centre = padded_rows[1:-1]
    columns = jnp.pad(centre, ((0, 0), (1, 1)), mode="edge")
    return (
        0.5 * (centre + padded_rows[:-2]),
        0.5 * (centre + padded_rows[2:]),
        0.5 * (centre + columns[:, :-2]),
        0.5 * (centre + columns[:, 2:]),
    )


def apply_faces(padded_rows, weights):
    north, south, west, east = weights
    centre = padded_rows[..., 1:-1, :]
    columns = jnp.pad(centre, [(0, 0)] * (centre.ndim - 1) + [(1, 1)])
    return (
        (north + south + west + east) * centre
        - north * padded_rows[..., :-2, :]
        - south * padded_rows[..., 2:, :]
        - west * columns[..., :-2]
        - east * columns[..., 2:]
    )


def borders_body(rank_ref, iterate_ref, forcing_ref, diff_ref, mine_ref, last_ref, done):
    steps, rows_dev, _ = iterate_ref.shape
    start = pl.multiple_of(jnp.where(rank_ref[0] == 0, rows_dev - PAD, 0), 8)
    copies = []
    for s in range(steps):
        copies.append((iterate_ref.at[s, pl.ds(start, PAD)], mine_ref.at[pl.ds(PAD * s, PAD)]))
        at = PAD * (steps + s)
        copies.append((forcing_ref.at[s, pl.ds(start, PAD)], mine_ref.at[pl.ds(at, PAD)]))
    copies.append((diff_ref.at[pl.ds(start, PAD)], mine_ref.at[pl.ds(2 * PAD * steps, PAD)]))
    copies.append((iterate_ref.at[steps - 1], last_ref))
    started = []
    for index, (source, target) in enumerate(copies):
        started.append(pltpu.make_async_copy(source, target, done.at[index]))
        started[-1].start()
    for copy in started:
        copy.wait()


def pack(out_ref, at, source_ref, slab, halo, flip=0):
    rows = slab + 2 * halo
    for target in range(out_ref.shape[0]):
        first = slab * target + PAD - halo
        for t in range(source_ref.shape[-1] // 128):
            out_ref[target ^ flip, at + rows * t : at + rows * (t + 1), :] = source_ref[
                first : first + rows, 128 * t : 128 * (t + 1)
            ]


def later_steps_body(slab, halo, rank_ref, wide_ref, pieces_ref):
    steps, _, columns = wide_ref.shape
    for s in range(1, steps):
        at = (s - 1) * (columns // 128) * (slab + 2 * halo)
        pack(pieces_ref, at, wide_ref.at[s], slab, halo, rank_ref[2])


def first_step_body(slab, halo, rank_ref, partial_ref, previous_ref, low_ref, high_ref,
                    pieces_ref, squares_ref, whole_ref):
    rows_dev, columns = previous_ref.shape
    keep_low = jnp.where(rank_ref[0] == 0, 0.0, 1.0)
    keep_high = jnp.where(rank_ref[0] == rank_ref[1] - 1, 0.0, 1.0)
    whole_ref[:PAD, :] = partial_ref[0, :PAD, :] + keep_low * low_ref[...]
    whole_ref[PAD + rows_dev :, :] = partial_ref[0, PAD + rows_dev :, :] + keep_high * high_ref[...]
    squares = jnp.zeros((8, columns), jnp.float32)
    for at in range(0, rows_dev, 8):
        value = partial_ref[0, PAD + at : PAD + at + 8, :] + previous_ref[at : at + 8, :]
        whole_ref[PAD + at : PAD + at + 8, :] = value
        squares = squares + value * value
    total = squares[:, :128]
    for t in range(1, columns // 128):
        total = total + squares[:, 128 * t : 128 * t + 128]
    squares_ref[0] = total
    pack(pieces_ref, 0, whole_ref, slab, halo)


def put_weights(diff_ref, south_ref, east_ref, west_ref):
    rows, columns = diff_ref.shape
    centre = diff_ref[...]
    below = jnp.concatenate([centre[1:], centre[-1:]], axis=0)
    lane = lax.broadcasted_iota(jnp.int32, (rows, columns), 1)
    after = jnp.where(lane == columns - 1, centre, pltpu.roll(centre, columns - 1, 1))
    quarter = 0.5 * time_step
    south = quarter * (centre + below)
    east = quarter * (centre + after)
    west = (2.0 * quarter) * centre[:, :128]
    for r in range(rows):
        south_ref[8 * r : 8 * r + 8, :] = jnp.broadcast_to(south[r : r + 1], (8, columns))
        east_ref[8 * r : 8 * r + 8, :] = jnp.broadcast_to(east[r : r + 1], (8, columns))
        west_ref[8 * r : 8 * r + 8, :] = jnp.broadcast_to(west[r : r + 1], (8, 128))


def transform(target, early_ref, late_ref, mix, rows, length, tiles):
    sources = early_ref.shape[0]
    steps_dev = length // sources
    starts = list(range(0, rows - 7, 8))
    if starts[-1] + 8 < rows:
        starts.append(rows - 8)
    for start in starts:
        for t in range(tiles):
            cells = []
            for source in range(sources):
                for step in range(steps_dev):
                    ref = late_ref if step == 0 else early_ref
                    at = (max(step - 1, 0) * tiles + t) * rows + start
                    cells.append(ref[source, at : at + 8, :])
            target[start * length : (start + 8) * length, 128 * t : 128 * t + 128] = jnp.dot(
                mix,
                jnp.concatenate(cells, axis=0),
                precision=lax.Precision.HIGHEST,
                preferred_element_type=jnp.float32,
            )


def krylov_body(length, slab, halo, sources, place_ref, late_ref, diff_ref, mix_ref, *rest):
    pieces = rest[:sources]
    vectors = rest[sources : sources + DEPTH]
    moments_ref, early_ref, south_ref, east_ref, west_ref = rest[sources + DEPTH :]
    rows = slab + 2 * halo
    columns = diff_ref.shape[-1]
    groups = length // 8
    tiles = columns // 128
    first_row = place_ref[0] + halo == 0
    last_row = place_ref[0] + halo + slab == place_ref[1]
    keep_above = jnp.where(first_row, 0.0, 1.0)
    keep_below = jnp.where(last_row, 0.0, 1.0)
    put_weights(diff_ref, south_ref, east_ref, west_ref)
    for index, piece in enumerate(pieces):
        early_ref[index ^ place_ref[2]] = piece[...]
    transform(vectors[0], early_ref, late_ref, mix_ref[...], rows, length, tiles)

    lane8 = lax.broadcasted_iota(jnp.int32, (8, 128), 1)
    is_first = lane8 == 0
    is_last = lane8 == 127

    def load(source, r, group):
        at = pl.multiple_of(r * length + 8 * group, 8)
        return [source[pl.ds(at, 8), 128 * t : 128 * t + 128] for t in range(tiles)]

    def row_of(ref, r, t):
        return ref[pl.ds(pl.multiple_of(8 * r, 8), 8), 128 * t : 128 * t + 128]

    def south_flux(r, here, under):
        return [row_of(south_ref, r, t) * (under[t] - here[t]) for t in range(tiles)]

    def stencil(r, here, under, north):
        south = south_flux(r, here, under)
        turned = [pltpu.roll(v, 127, 1) for v in here] + [0.0]
        east = [
            row_of(east_ref, r, t) * (jnp.where(is_last, turned[t + 1], turned[t]) - here[t])
            for t in range(tiles)
        ]
        moved = [row_of(west_ref, r, 0) * here[0]] + [pltpu.roll(f, 1, 1) for f in east]
        value = [
            (jnp.where(is_first, moved[t], moved[t + 1]) - east[t]) + (north[t] - south[t])
            for t in range(tiles)
        ]
        return value, south

    def total(parts):
        while len(parts) > 1:
            parts = [parts[i] + parts[i + 1] for i in range(0, len(parts) - 1, 2)] + (
                [parts[-1]] if len(parts) % 2 else []
            )
        return parts[0]

    table = [jnp.zeros((8, 128), jnp.float32) for _ in range(groups)]

    def put(entry, index, sums):
        return jnp.where(lane8 == index, jnp.sum(sums, axis=1, keepdims=True), entry)

    for power in range(DEPTH):
        source = vectors[power]
        target = vectors[power + 1] if power + 1 < DEPTH else None
        first, final = power + 1, rows - 1 - power
        for group in range(groups):

            def step(r, carry, summing):
                here, north, sums = carry
                under = load(source, r + 1, group)
                value, south = stencil(r, here, under, north)
                if target is not None:
                    at = pl.multiple_of(r * length + 8 * group, 8)
                    for t in range(tiles):
                        target[pl.ds(at, 8), 128 * t : 128 * t + 128] = value[t]
                if summing:
                    products = [
                        sums[0] + total([v * v for v in here]),
                        sums[1] + total([v * w for v, w in zip(here, value)]),
                    ]
                    if target is None:
                        products.append(sums[2] + total([w * w for w in value]))
                    sums = tuple(products)
                return tuple(under), tuple(south), sums

            top = load(source, first - 1, group)
            here = load(source, first, group)
            carry = (tuple(here), tuple(south_flux(first - 1, top, here)), ())
            if first < halo:
                carry = lax.fori_loop(
                    first, halo, functools.partial(step, summing=False), carry, unroll=True
                )
            zero = jnp.zeros((8, 128), jnp.float32)
            carry = (carry[0], carry[1], (zero,) * (2 if target is not None else 3))
            carry = lax.fori_loop(
                halo, halo + slab, functools.partial(step, summing=True), carry, unroll=min(UNROLL, max(1, slab // 2))
            )
            for index, sums in enumerate(carry[2]):
                table[group] = put(table[group], 2 * power + index, sums)
            if first < halo:
                carry = (carry[0], carry[1], ())
                lax.fori_loop(
                    halo + slab, final, functools.partial(step, summing=False), carry, unroll=True
                )
            if target is not None and first < halo:
                for r, keep in ((halo - 1, keep_above), (halo + slab, keep_below)):
                    at = r * length + 8 * group
                    target[at : at + 8, :] = target[at : at + 8, :] * keep
    moments_ref[...] = jnp.concatenate(table, axis=0)


def combine_body(length, slab, halo, moments_ref, table_ref, shift_ref, mix_ref, *rest):
    power_refs = rest[:DEPTH]
    out_ref = rest[DEPTH]
    steps_dev = out_ref.shape[1] // slab
    half = length // 2
    own = moments_ref[...]
    swapped = jnp.concatenate([own[half:], own[:half]], axis=0)
    channel = lax.broadcasted_iota(jnp.int32, own.shape, 0)
    alone = (channel == 0) | (channel == half)
    sums = jnp.where(alone, own, own + swapped)
    mu = [
        jnp.sum(sums * table_ref[k + 1], axis=1, keepdims=True) for k in range(2 * CG_ITERS)
    ]
    low1, low2 = mu[2] / mu[1], mu[3] / mu[1]
    pivot1 = mu[3] - low1 * mu[2]
    cross = mu[4] - low1 * mu[3]
    pivot2 = mu[5] - low2 * mu[3]
    right1 = mu[1] - low1 * mu[0]
    right2 = mu[2] - low2 * mu[0]
    low3 = cross / pivot1
    pivot2 = pivot2 - low3 * cross
    right2 = right2 - low3 * right1
    c2 = right2 / pivot2
    c1 = (right1 - cross * c2) / pivot1
    c0 = (mu[0] - mu[2] * c1 - mu[3] * c2) / mu[1]
    inner = c0 * table_ref[0] + c1 * table_ref[1] + c2 * table_ref[2]
    real = shift_ref[0]
    imag = shift_ref[1]
    lanes = lax.broadcasted_iota(jnp.int32, inner.shape, 1)
    outer = real * inner + jnp.where(lanes == 0, 0.0, pltpu.roll(inner, 1, 1))
    crossed = imag * inner
    sign = jnp.where(lax.broadcasted_iota(jnp.int32, inner.shape, 0) < half, 1.0, -1.0)
    crossed = sign * crossed
    columns = out_ref.shape[-1]

    def spread(values, index):
        return jnp.broadcast_to(values[:, index : index + 1], (length, columns))[None]

    for start in range(0, slab, 8):
        total = jnp.zeros((8, length, columns), jnp.float32)
        other = jnp.zeros((8, length, columns), jnp.float32)
        for power in range(DEPTH):
            at = (halo + start) * length
            here = power_refs[power][at : at + 8 * length, :].reshape(8, length, columns)
            total = total + spread(outer, power) * here
            if power + 1 < DEPTH:
                flipped = jnp.concatenate([here[:, half:], here[:, :half]], axis=1)
                other = other + spread(crossed, power) * flipped
        block = (total + other).reshape(8 * length, columns)
        result = jnp.dot(
            mix_ref[...], block, precision=lax.Precision.HIGHEST, preferred_element_type=jnp.float32
        )
        for step in range(length):
            at = (step % steps_dev) * slab + start
            out_ref[step // steps_dev, at : at + 8, :] = result[step * 8 : step * 8 + 8]


def iteration(iterate, forcing, initial_state, diffusivity):
    steps_dev, rows_dev, columns_dev = iterate.shape
    time_devices = lax.axis_size("tm")
    row_devices = lax.axis_size("rows")
    time_rank = lax.axis_index("tm")
    row_rank = lax.axis_index("rows")
    length = steps_dev * time_devices
    cell_count = rows_dev * row_devices * columns_dev
    slab = rows_dev // time_devices
    halo = DEPTH
    rows = slab + 2 * halo

    tiles = columns_dev // 128
    vmem = pl.BlockSpec(memory_space=pltpu.VMEM)
    smem = pl.BlockSpec(memory_space=pltpu.SMEM)
    params = pltpu.CompilerParams(vmem_limit_bytes=24 * 2**20)
    rank = jnp.stack([row_rank, jnp.int32(row_devices), time_rank]).astype(jnp.int32)

    if row_devices == 2:
        mine, last = pl.pallas_call(
            borders_body,
            out_shape=[
                pltpu.VMEM(((2 * steps_dev + 1) * PAD, columns_dev), jnp.float32),
                pltpu.VMEM((rows_dev, columns_dev), jnp.float32),
            ],
            in_specs=[smem] + [pl.BlockSpec(memory_space=pltpu.HBM)] * 3,
            out_specs=[vmem] * 2,
            scratch_shapes=[pltpu.SemaphoreType.DMA((2 * steps_dev + 2,))],
            compiler_params=pltpu.CompilerParams(vmem_limit_bytes=2**26 - 3 * 2**18),
            name="borders",
        )(rank, iterate, forcing, diffusivity)
        low = high = lax.ppermute(mine, "rows", [(0, 1), (1, 0)])
    else:
        last = iterate[-1]
        low, high = border_rows((iterate, forcing, diffusivity), "rows", PAD)
    arriving = from_behind(last, "tm", 1)

    keep_low = jnp.where(row_rank == 0, 0.0, 1.0)
    keep_high = jnp.where(row_rank == row_devices - 1, 0.0, 1.0)

    def widened(block, slot):
        shape = (steps_dev, PAD, columns_dev)
        at = slice(slot * PAD, (slot + steps_dev) * PAD)
        return jnp.concatenate(
            [keep_low * low[at].reshape(shape), block, keep_high * high[at].reshape(shape)], axis=1
        )

    diff_low = jnp.where(row_rank == 0, diffusivity[:1], low[-PAD:])
    diff_high = jnp.where(row_rank == row_devices - 1, diffusivity[-1:], high[-PAD:])
    rimmed = jnp.concatenate([diff_low, diffusivity, diff_high])
    wide_iterate = widened(iterate, 0)
    faces = face_weights(jnp.pad(rimmed, ((1, 1), (0, 0)), mode="edge"))
    wide_rows = jnp.pad(wide_iterate, ((0, 0), (1, 1), (0, 0)))
    wide = time_step * (widened(forcing, steps_dev) - apply_faces(wide_rows, faces)) - wide_iterate
    wide = wide + jnp.concatenate([jnp.zeros_like(wide_iterate[:1]), wide_iterate[:-1]])
    at_row = lax.broadcasted_iota(jnp.int32, (1, rows_dev + 2 * PAD, 1), 1)
    keep = jnp.where(at_row < PAD, keep_low, jnp.where(at_row < PAD + rows_dev, 1.0, keep_high))
    wide = wide * keep
    own = wide[1:, PAD : PAD + rows_dev]
    squares_late = jnp.sum(own * own, axis=(1, 2))

    padded = rows_dev + 2 * PAD
    early = pl.pallas_call(
        functools.partial(later_steps_body, slab, halo),
        out_shape=jax.ShapeDtypeStruct(
            (time_devices, (steps_dev - 1) * tiles * rows, 128), jnp.float32
        ),
        in_specs=[smem, vmem],
        out_specs=vmem,
        compiler_params=params,
        name="later_steps",
    )(rank, wide)
    early = exchanged(early)

    previous = jnp.where(time_rank == 0, initial_state, arriving)
    before_low, before_high = border_rows((previous,), "rows", PAD)
    late, squares_first = pl.pallas_call(
        functools.partial(first_step_body, slab, halo),
        out_shape=[
            jax.ShapeDtypeStruct((time_devices, tiles * rows, 128), jnp.float32),
            jax.ShapeDtypeStruct((1, 8, 128), jnp.float32),
        ],
        in_specs=[smem] + [vmem] * 4,
        out_specs=[vmem] * 2,
        scratch_shapes=[pltpu.VMEM((padded, columns_dev), jnp.float32)],
        compiler_params=params,
        name="first_step",
    )(rank, wide, previous, before_low, before_high)
    late = lax.all_to_all(late, "tm", split_axis=0, concat_axis=0, tiled=True)

    squares = jnp.concatenate([jnp.sum(squares_first, axis=(1, 2)), squares_late])
    residual_rms = jnp.sqrt(lax.psum(squares, "rows") / cell_count + rms_eps)

    diff_slab = lax.dynamic_slice_in_dim(rimmed, slab * time_rank + PAD - halo, rows, axis=0)
    place = jnp.stack(
        [
            row_rank * rows_dev + time_rank * slab - halo,
            jnp.int32(rows_dev * row_devices),
            time_rank,
        ]
    ).astype(jnp.int32)

    vector = pltpu.VMEM((rows * length, columns_dev), jnp.float32)
    *powers, moments = pl.pallas_call(
        functools.partial(krylov_body, length, slab, halo, time_devices),
        out_shape=[vector] * DEPTH + [jax.ShapeDtypeStruct((length, 128), jnp.float32)],
        in_specs=[smem] + [vmem] * (3 + time_devices),
        out_specs=[vmem] * (DEPTH + 1),
        scratch_shapes=[
            pltpu.VMEM((time_devices, (steps_dev - 1) * tiles * rows, 128), jnp.float32),
            pltpu.VMEM((rows * 8, columns_dev), jnp.float32),
            pltpu.VMEM((rows * 8, columns_dev), jnp.float32),
            pltpu.VMEM((rows * 8, 128), jnp.float32),
        ],
        compiler_params=params,
        name="krylov",
    )(place, late, diff_slab, jnp.asarray(block_forward(length, 8)), *early)

    for axis in ("rows", "tm"):
        count = lax.axis_size(axis)
        if count & (count - 1):
            moments = lax.psum(moments, axis)
        else:
            step = 1
            while step < count:
                pairs = [(i, i ^ step) for i in range(count)]
                moments = moments + lax.ppermute(moments, axis, pairs)
                step *= 2

    real, imag = channel_shifts(length)
    shift = np.broadcast_to(np.stack([real, imag])[:, :, None], (2, length, 128))
    table = np.zeros((DEPTH + 1, length, 128))
    table[:, :, :MOMENTS] = power_table(length)
    corrected = pl.pallas_call(
        functools.partial(combine_body, length, slab, halo),
        out_shape=jax.ShapeDtypeStruct((time_devices, steps_dev * slab, columns_dev), jnp.float32),
        in_specs=[vmem] * (4 + DEPTH),
        out_specs=vmem,
        compiler_params=params,
        name="combine",
    )(
        moments,
        jnp.asarray(table, jnp.float32),
        jnp.asarray(shift, jnp.float32),
        jnp.asarray(block_inverse(length, 8)),
        *powers,
    )
    back = lax.all_to_all(corrected, "tm", split_axis=0, concat_axis=0, tiled=True)
    own_steps = back.reshape(time_devices, steps_dev, slab, columns_dev)
    own_steps = jnp.swapaxes(own_steps, 0, 1).reshape(steps_dev, rows_dev, columns_dev)
    updated = iterate + own_steps
    return (updated, residual_rms)


def solution(mesh):
    placed = (
        P(("groups", "tm"), "rows", None),
        P(("groups", "tm"), "rows", None),
        P(("groups", "rows"), None),
        P(("groups", "rows"), None),
    )
    return jax.shard_map(
        iteration,
        mesh=mesh,
        in_specs=placed,
        out_specs=(P(("groups", "tm"), "rows", None), P(("groups", "tm"))),
        check_vma=False,
    )
```

```python
import functools
import math

import jax
import jax.numpy as jnp
import numpy as np
from jax import lax
from jax.experimental import pallas as pl
from jax.experimental.pallas import tpu as pltpu
from jax.sharding import PartitionSpec as P


CG_ITERS = 3
DEPTH = 2 * CG_ITERS
MOMENTS = 2 * DEPTH + 1
UNROLL = 16
LEAST_PIVOTS = (2e-2, 2e-3)
PAD = 8

circulant_alpha = 0.05
time_step = 0.5
rms_eps = 1e-06


def from_behind(value, axis, steps):
    count = lax.axis_size(axis)
    initial, last = (max(0, -steps), min(count, count - steps))
    return lax.ppermute(value, axis, [(source, source + steps) for source in range(initial, last)])


def exchanged(pieces):
    count = pieces.shape[0]
    got = [pieces[0]] + [None] * (count - 1)
    for k in reversed(range(1, count)):
        got[k] = lax.ppermute(pieces[k], "tm", [(i, i ^ k) for i in range(count)])
    return got


def summed_over_group(values):
    for axis in ("rows", "tm"):
        count = lax.axis_size(axis)
        if count & (count - 1):
            values = lax.psum(values, axis)
        else:
            step = 1
            while step < count:
                pairs = [(i, i ^ step) for i in range(count)]
                values = values + lax.ppermute(values, axis, pairs)
                step *= 2
    return values


def extended(block, axis, dim, width):
    count = lax.axis_size(axis)
    forward = [(i, i + 1) for i in range(count - 1)]
    backward = [(target, source) for source, target in forward]
    low = lax.slice_in_dim(block, block.shape[dim] - width, None, axis=dim)
    high = lax.slice_in_dim(block, 0, width, axis=dim)
    low, high = lax.ppermute(low, axis, forward), lax.ppermute(high, axis, backward)
    return jnp.concatenate([low, block, high], axis=dim)


def careful_correction(iterate, forcing, initial_state, diffusivity):
    steps_dev, rows_dev, columns = iterate.shape
    time_devices = lax.axis_size("tm")
    row_devices = lax.axis_size("rows")
    time_rank = lax.axis_index("tm")
    row_rank = lax.axis_index("rows")
    length = steps_dev * time_devices
    half = length // 2
    slab = rows_dev // time_devices
    halo = -(-(DEPTH + 1) // 8) * 8
    rows = slab + 2 * halo
    rimmed = extended(diffusivity, "rows", 0, halo)
    at = lax.broadcasted_iota(jnp.int32, (rows_dev + 2 * halo, 1), 0)
    rimmed = jnp.where((row_rank == 0) & (at < halo), diffusivity[:1], rimmed)
    beyond = (row_rank == row_devices - 1) & (at >= halo + rows_dev)
    rimmed = jnp.where(beyond, diffusivity[-1:], rimmed)
    arriving = from_behind(iterate[-1], "tm", 1)
    first_previous = jnp.where(time_rank == 0, initial_state, arriving)
    previous = jnp.concatenate([first_previous[None], iterate[:-1]], axis=0)
    faces = face_weights(rimmed[halo - 1 : halo + rows_dev + 1])
    spread = apply_faces(extended(iterate, "rows", 1, 1), faces)
    residual = time_step * forcing + previous - iterate - time_step * spread
    wide = extended(residual, "rows", 1, halo)
    pieces = jnp.stack(
        [lax.slice_in_dim(wide, slab * k, slab * k + rows, axis=1) for k in range(time_devices)]
    )
    pieces = lax.all_to_all(pieces, "tm", split_axis=0, concat_axis=0, tiled=True)
    flat = pieces.reshape(length, rows * columns)
    spectrum = jnp.dot(
        jnp.asarray(forward_matrix(length), jnp.float32), flat, precision=lax.Precision.HIGHEST
    ).reshape(length, rows, columns)

    slab_faces = face_weights(
        jnp.pad(
            lax.dynamic_slice_in_dim(rimmed, slab * time_rank, rows, axis=0),
            ((1, 1), (0, 0)),
            mode="edge",
        )
    )
    place = lax.broadcasted_iota(jnp.int32, (1, rows, 1), 1) - halo
    grid_row = place + row_rank * rows_dev + time_rank * slab
    inside = (grid_row >= 0) & (grid_row < rows_dev * row_devices)
    own = (place >= 0) & (place < slab)
    real, imag = channel_shifts(length)
    real = jnp.asarray(real[:, None, None], jnp.float32)
    imag = jnp.asarray(imag[:, None, None], jnp.float32)
    channel = lax.broadcasted_iota(jnp.int32, (length, 1, 1), 0)
    alone = (channel == 0) | (channel == half)

    def operate(values, orientation):
        padded = jnp.pad(values, ((0, 0), (1, 1), (0, 0)))
        spread = time_step * apply_faces(padded, slab_faces)
        swapped = jnp.concatenate([-values[half:], values[:half]])
        return jnp.where(inside, real * values + orientation * imag * swapped + spread, 0.0)

    def norm(values):
        sums = jnp.sum(jnp.where(own, values * values, 0.0), axis=(1, 2), keepdims=True)
        sums = summed_over_group(sums)
        return jnp.where(alone, sums, sums + jnp.concatenate([sums[half:], sums[:half]]))

    def iterated(_, state):
        result, remain, search, gamma = state
        image = operate(search, 1.0)
        rate = gamma / norm(image)
        result = result + rate * search
        remain = remain - rate * image
        normal = operate(remain, -1.0)
        gamma_next = norm(normal)
        search = normal + (gamma_next / gamma) * search
        return result, remain, search, gamma_next

    normal = operate(spectrum, -1.0)
    state = (jnp.zeros_like(spectrum), spectrum, normal, norm(normal))
    result = lax.fori_loop(0, CG_ITERS, iterated, state)[0]
    result = result[:, halo : halo + slab].reshape(length, slab * columns)
    corrected = jnp.dot(
        jnp.asarray(inverse_matrix(length), jnp.float32), result, precision=lax.Precision.HIGHEST
    ).reshape(time_devices, steps_dev * slab, columns)
    return lax.all_to_all(corrected, "tm", split_axis=0, concat_axis=0, tiled=True)


def border_rows(blocks, axis, width):
    count = lax.axis_size(axis)
    if count == 2:
        first = lax.axis_index(axis) == 0

        def edge(block):
            return jnp.where(first, block[..., -width:, :], block[..., :width, :])

        mine = jnp.concatenate([edge(block).reshape(-1, block.shape[-1]) for block in blocks])
        got = lax.ppermute(mine, axis, [(0, 1), (1, 0)])
        return got, got
    low = jnp.concatenate([b[..., -width:, :].reshape(-1, b.shape[-1]) for b in blocks])
    high = jnp.concatenate([b[..., :width, :].reshape(-1, b.shape[-1]) for b in blocks])
    return (
        lax.ppermute(low, axis, [(i, i + 1) for i in range(count - 1)]),
        lax.ppermute(high, axis, [(i + 1, i) for i in range(count - 1)]),
    )


def growth_of(length):
    return np.exp(math.log(circulant_alpha) * np.arange(length) / length)


def forward_matrix(length):
    half = length // 2
    steps = np.arange(length)
    table = np.zeros((length, length))
    for j in range(half):
        turn = 2 * np.pi * ((j * steps) % length) / length
        table[j] = np.cos(turn)
        table[half + j] = -np.sin(turn)
    table[half] = np.cos(2 * np.pi * ((half * steps) % length) / length)
    return table * growth_of(length)[None, :]


def inverse_matrix(length):
    half = length // 2
    steps = np.arange(length)
    table = np.zeros((length, length))
    for j in range(half):
        turn = 2 * np.pi * ((j * steps) % length) / length
        weight = 1.0 if j == 0 else 2.0
        table[:, j] = weight * np.cos(turn) / length
        table[:, half + j] = -weight * np.sin(turn) / length
    table[:, half] = np.cos(2 * np.pi * ((half * steps) % length) / length) / length
    return table / growth_of(length)[:, None]


def block_forward(length, rows):
    full = np.einsum("cn,rs->rcns", forward_matrix(length), np.eye(rows))
    return full.reshape(rows * length, length * rows).astype(np.float32)


def block_inverse(length, rows):
    full = np.einsum("nc,rs->nrsc", inverse_matrix(length), np.eye(rows))
    return full.reshape(length * rows, rows * length).astype(np.float32)


def channel_shifts(length):
    half = length // 2
    root = math.exp(math.log(circulant_alpha) / length)
    freq = np.concatenate([np.arange(half), np.arange(half)])
    freq[half] = half
    angle = 2 * np.pi * freq / length
    real = 1 - root * np.cos(angle)
    imag = root * np.sin(angle)
    imag[0] = 0.0
    imag[half] = 0.0
    return real, imag


def power_table(length):
    real, imag = channel_shifts(length)
    base = np.stack([real**2 + imag**2, 2 * real, np.ones_like(real)], axis=1)
    powers = [np.concatenate([np.ones((length, 1)), np.zeros((length, MOMENTS - 1))], axis=1)]
    for _ in range(DEPTH):
        last = powers[-1]
        following = np.zeros_like(last)
        for m in range(3):
            following[:, m:] += base[:, m : m + 1] * last[:, : MOMENTS - m]
        powers.append(following)
    return np.stack(powers)


def face_weights(padded_rows):
    centre = padded_rows[1:-1]
    columns = jnp.pad(centre, ((0, 0), (1, 1)), mode="edge")
    return (
        0.5 * (centre + padded_rows[:-2]),
        0.5 * (centre + padded_rows[2:]),
        0.5 * (centre + columns[:, :-2]),
        0.5 * (centre + columns[:, 2:]),
    )


def apply_faces(padded_rows, weights):
    north, south, west, east = weights
    centre = padded_rows[..., 1:-1, :]
    columns = jnp.pad(centre, [(0, 0)] * (centre.ndim - 1) + [(1, 1)])
    return (
        (north + south + west + east) * centre
        - north * padded_rows[..., :-2, :]
        - south * padded_rows[..., 2:, :]
        - west * columns[..., :-2]
        - east * columns[..., 2:]
    )


def borders_body(rank_ref, iterate_ref, forcing_ref, diff_ref, mine_ref, last_ref, done):
    steps, rows_dev, _ = iterate_ref.shape
    start = pl.multiple_of(jnp.where(rank_ref[0] == 0, rows_dev - PAD, 0), 8)
    copies = []
    for s in range(steps):
        copies.append((iterate_ref.at[s, pl.ds(start, PAD)], mine_ref.at[pl.ds(PAD * s, PAD)]))
        at = PAD * (steps + s)
        copies.append((forcing_ref.at[s, pl.ds(start, PAD)], mine_ref.at[pl.ds(at, PAD)]))
    copies.append((diff_ref.at[pl.ds(start, PAD)], mine_ref.at[pl.ds(2 * PAD * steps, PAD)]))
    copies.append((iterate_ref.at[steps - 1], last_ref))
    started = []
    for index, (source, target) in enumerate(copies):
        started.append(pltpu.make_async_copy(source, target, done.at[index]))
        started[-1].start()
    for copy in started:
        copy.wait()


def pack(out_ref, at, source_ref, slab, halo, flip=0):
    rows = slab + 2 * halo
    for target in range(out_ref.shape[0]):
        first = slab * target + PAD - halo
        for t in range(source_ref.shape[-1] // 128):
            out_ref[target ^ flip, at + rows * t : at + rows * (t + 1), :] = source_ref[
                first : first + rows, 128 * t : 128 * (t + 1)
            ]


def later_steps_body(slab, halo, rank_ref, wide_ref, pieces_ref):
    steps, _, columns = wide_ref.shape
    for s in range(1, steps):
        at = (s - 1) * (columns // 128) * (slab + 2 * halo)
        pack(pieces_ref, at, wide_ref.at[s], slab, halo, rank_ref[2])


def first_step_body(slab, halo, rank_ref, partial_ref, previous_ref, low_ref, high_ref,
                    pieces_ref, squares_ref, whole_ref):
    rows_dev, columns = previous_ref.shape
    keep_low = jnp.where(rank_ref[0] == 0, 0.0, 1.0)
    keep_high = jnp.where(rank_ref[0] == rank_ref[1] - 1, 0.0, 1.0)
    whole_ref[:PAD, :] = partial_ref[0, :PAD, :] + keep_low * low_ref[...]
    whole_ref[PAD + rows_dev :, :] = partial_ref[0, PAD + rows_dev :, :] + keep_high * high_ref[...]
    squares = jnp.zeros((8, columns), jnp.float32)
    for at in range(0, rows_dev, 8):
        value = partial_ref[0, PAD + at : PAD + at + 8, :] + previous_ref[at : at + 8, :]
        whole_ref[PAD + at : PAD + at + 8, :] = value
        squares = squares + value * value
    total = squares[:, :128]
    for t in range(1, columns // 128):
        total = total + squares[:, 128 * t : 128 * t + 128]
    squares_ref[0] = total
    pack(pieces_ref, 0, whole_ref, slab, halo)


def put_weights(diff_ref, south_ref, east_ref, west_ref):
    rows, columns = diff_ref.shape
    centre = diff_ref[...]
    below = jnp.concatenate([centre[1:], centre[-1:]], axis=0)
    lane = lax.broadcasted_iota(jnp.int32, (rows, columns), 1)
    after = jnp.where(lane == columns - 1, centre, pltpu.roll(centre, columns - 1, 1))
    quarter = 0.5 * time_step
    south = quarter * (centre + below)
    east = quarter * (centre + after)
    west = (2.0 * quarter) * centre[:, :128]
    for r in range(rows):
        south_ref[8 * r : 8 * r + 8, :] = jnp.broadcast_to(south[r : r + 1], (8, columns))
        east_ref[8 * r : 8 * r + 8, :] = jnp.broadcast_to(east[r : r + 1], (8, columns))
        west_ref[8 * r : 8 * r + 8, :] = jnp.broadcast_to(west[r : r + 1], (8, 128))


def transform(target, early_ref, late_ref, mix, rows, length, tiles):
    sources = early_ref.shape[0]
    steps_dev = length // sources
    starts = list(range(0, rows - 7, 8))
    if starts[-1] + 8 < rows:
        starts.append(rows - 8)
    for start in starts:
        for t in range(tiles):
            cells = []
            for source in range(sources):
                for step in range(steps_dev):
                    ref = late_ref if step == 0 else early_ref
                    at = (max(step - 1, 0) * tiles + t) * rows + start
                    cells.append(ref[source, at : at + 8, :])
            target[start * length : (start + 8) * length, 128 * t : 128 * t + 128] = jnp.dot(
                mix,
                jnp.concatenate(cells, axis=0),
                precision=lax.Precision.HIGHEST,
                preferred_element_type=jnp.float32,
            )


def krylov_body(length, slab, halo, sources, place_ref, late_ref, diff_ref, mix_ref, *rest):
    pieces = rest[:sources]
    vectors = rest[sources : sources + DEPTH]
    moments_ref, early_ref, south_ref, east_ref, west_ref = rest[sources + DEPTH :]
    rows = slab + 2 * halo
    columns = diff_ref.shape[-1]
    groups = length // 8
    tiles = columns // 128
    first_row = place_ref[0] + halo == 0
    last_row = place_ref[0] + halo + slab == place_ref[1]
    keep_above = jnp.where(first_row, 0.0, 1.0)
    keep_below = jnp.where(last_row, 0.0, 1.0)
    put_weights(diff_ref, south_ref, east_ref, west_ref)
    for index, piece in enumerate(pieces):
        early_ref[index ^ place_ref[2]] = piece[...]
    transform(vectors[0], early_ref, late_ref, mix_ref[...], rows, length, tiles)

    lane8 = lax.broadcasted_iota(jnp.int32, (8, 128), 1)
    is_first = lane8 == 0
    is_last = lane8 == 127

    def load(source, r, group):
        at = pl.multiple_of(r * length + 8 * group, 8)
        return [source[pl.ds(at, 8), 128 * t : 128 * t + 128] for t in range(tiles)]

    def row_of(ref, r, t):
        return ref[pl.ds(pl.multiple_of(8 * r, 8), 8), 128 * t : 128 * t + 128]

    def south_flux(r, here, under):
        return [row_of(south_ref, r, t) * (under[t] - here[t]) for t in range(tiles)]

    def stencil(r, here, under, north):
        south = south_flux(r, here, under)
        turned = [pltpu.roll(v, 127, 1) for v in here] + [0.0]
        east = [
            row_of(east_ref, r, t) * (jnp.where(is_last, turned[t + 1], turned[t]) - here[t])
            for t in range(tiles)
        ]
        moved = [row_of(west_ref, r, 0) * here[0]] + [pltpu.roll(f, 1, 1) for f in east]
        value = [
            (jnp.where(is_first, moved[t], moved[t + 1]) - east[t]) + (north[t] - south[t])
            for t in range(tiles)
        ]
        return value, south

    def total(parts):
        while len(parts) > 1:
            parts = [parts[i] + parts[i + 1] for i in range(0, len(parts) - 1, 2)] + (
                [parts[-1]] if len(parts) % 2 else []
            )
        return parts[0]

    table = [jnp.zeros((8, 128), jnp.float32) for _ in range(groups)]

    def put(entry, index, sums):
        return jnp.where(lane8 == index, jnp.sum(sums, axis=1, keepdims=True), entry)

    for power in range(DEPTH):
        source = vectors[power]
        target = vectors[power + 1] if power + 1 < DEPTH else None
        first, final = power + 1, rows - 1 - power
        for group in range(groups):

            def step(r, carry, summing):
                here, north, sums = carry
                under = load(source, r + 1, group)
                value, south = stencil(r, here, under, north)
                if target is not None:
                    at = pl.multiple_of(r * length + 8 * group, 8)
                    for t in range(tiles):
                        target[pl.ds(at, 8), 128 * t : 128 * t + 128] = value[t]
                if summing:
                    products = [
                        sums[0] + total([v * v for v in here]),
                        sums[1] + total([v * w for v, w in zip(here, value)]),
                    ]
                    if target is None:
                        products.append(sums[2] + total([w * w for w in value]))
                    sums = tuple(products)
                return tuple(under), tuple(south), sums

            top = load(source, first - 1, group)
            here = load(source, first, group)
            carry = (tuple(here), tuple(south_flux(first - 1, top, here)), ())
            if first < halo:
                carry = lax.fori_loop(
                    first, halo, functools.partial(step, summing=False), carry, unroll=True
                )
            zero = jnp.zeros((8, 128), jnp.float32)
            carry = (carry[0], carry[1], (zero,) * (2 if target is not None else 3))
            carry = lax.fori_loop(
                halo, halo + slab, functools.partial(step, summing=True), carry, unroll=min(UNROLL, max(1, slab // 2))
            )
            for index, sums in enumerate(carry[2]):
                table[group] = put(table[group], 2 * power + index, sums)
            if first < halo:
                carry = (carry[0], carry[1], ())
                lax.fori_loop(
                    halo + slab, final, functools.partial(step, summing=False), carry, unroll=True
                )
            if target is not None and first < halo:
                for r, keep in ((halo - 1, keep_above), (halo + slab, keep_below)):
                    at = r * length + 8 * group
                    target[at : at + 8, :] = target[at : at + 8, :] * keep
    moments_ref[...] = jnp.concatenate(table, axis=0)


def combine_body(length, slab, halo, moments_ref, table_ref, shift_ref, mix_ref, *rest):
    power_refs = rest[:DEPTH]
    out_ref, doubt_ref = rest[DEPTH:]
    steps_dev = out_ref.shape[1] // slab
    half = length // 2
    own = moments_ref[...]
    swapped = jnp.concatenate([own[half:], own[:half]], axis=0)
    channel = lax.broadcasted_iota(jnp.int32, own.shape, 0)
    alone = (channel == 0) | (channel == half)
    sums = jnp.where(alone, own, own + swapped)
    mu = [
        jnp.sum(sums * table_ref[k + 1], axis=1, keepdims=True) for k in range(2 * CG_ITERS)
    ]
    low1, low2 = mu[2] / mu[1], mu[3] / mu[1]
    pivot1 = mu[3] - low1 * mu[2]
    cross = mu[4] - low1 * mu[3]
    pivot2 = mu[5] - low2 * mu[3]
    right1 = mu[1] - low1 * mu[0]
    right2 = mu[2] - low2 * mu[0]
    low3 = cross / pivot1
    pivot2 = pivot2 - low3 * cross
    right2 = right2 - low3 * right1
    sound = (pivot1 > LEAST_PIVOTS[0] * mu[3]) & (pivot2 > LEAST_PIVOTS[1] * mu[5])
    doubt = jnp.max(jnp.where(sound, 0.0, 1.0), axis=0, keepdims=True)
    doubt_ref[...] = jnp.broadcast_to(doubt, doubt_ref.shape)
    c2 = right2 / pivot2
    c1 = (right1 - cross * c2) / pivot1
    c0 = (mu[0] - mu[2] * c1 - mu[3] * c2) / mu[1]
    inner = c0 * table_ref[0] + c1 * table_ref[1] + c2 * table_ref[2]
    real = shift_ref[0]
    imag = shift_ref[1]
    lanes = lax.broadcasted_iota(jnp.int32, inner.shape, 1)
    outer = real * inner + jnp.where(lanes == 0, 0.0, pltpu.roll(inner, 1, 1))
    crossed = imag * inner
    sign = jnp.where(lax.broadcasted_iota(jnp.int32, inner.shape, 0) < half, 1.0, -1.0)
    crossed = sign * crossed
    columns = out_ref.shape[-1]

    def spread(values, index):
        return jnp.broadcast_to(values[:, index : index + 1], (length, columns))[None]

    for start in range(0, slab, 8):
        total = jnp.zeros((8, length, columns), jnp.float32)
        other = jnp.zeros((8, length, columns), jnp.float32)
        for power in range(DEPTH):
            at = (halo + start) * length
            here = power_refs[power][at : at + 8 * length, :].reshape(8, length, columns)
            total = total + spread(outer, power) * here
            if power + 1 < DEPTH:
                flipped = jnp.concatenate([here[:, half:], here[:, :half]], axis=1)
                other = other + spread(crossed, power) * flipped
        block = (total + other).reshape(8 * length, columns)
        result = jnp.dot(
            mix_ref[...], block, precision=lax.Precision.HIGHEST, preferred_element_type=jnp.float32
        )
        for step in range(length):
            at = (step % steps_dev) * slab + start
            out_ref[step // steps_dev, at : at + 8, :] = result[step * 8 : step * 8 + 8]


def iteration(iterate, forcing, initial_state, diffusivity):
    steps_dev, rows_dev, columns_dev = iterate.shape
    time_devices = lax.axis_size("tm")
    row_devices = lax.axis_size("rows")
    time_rank = lax.axis_index("tm")
    row_rank = lax.axis_index("rows")
    length = steps_dev * time_devices
    cell_count = rows_dev * row_devices * columns_dev
    slab = rows_dev // time_devices
    halo = DEPTH
    rows = slab + 2 * halo

    tiles = columns_dev // 128
    vmem = pl.BlockSpec(memory_space=pltpu.VMEM)
    smem = pl.BlockSpec(memory_space=pltpu.SMEM)
    params = pltpu.CompilerParams(vmem_limit_bytes=24 * 2**20)
    rank = jnp.stack([row_rank, jnp.int32(row_devices), time_rank]).astype(jnp.int32)

    if row_devices == 2:
        mine, last = pl.pallas_call(
            borders_body,
            out_shape=[
                pltpu.VMEM(((2 * steps_dev + 1) * PAD, columns_dev), jnp.float32),
                pltpu.VMEM((rows_dev, columns_dev), jnp.float32),
            ],
            in_specs=[smem] + [pl.BlockSpec(memory_space=pltpu.HBM)] * 3,
            out_specs=[vmem] * 2,
            scratch_shapes=[pltpu.SemaphoreType.DMA((2 * steps_dev + 2,))],
            compiler_params=pltpu.CompilerParams(vmem_limit_bytes=2**26 - 3 * 2**18),
            name="borders",
        )(rank, iterate, forcing, diffusivity)
        low = high = lax.ppermute(mine, "rows", [(0, 1), (1, 0)])
    else:
        last = iterate[-1]
        low, high = border_rows((iterate, forcing, diffusivity), "rows", PAD)
    arriving = from_behind(last, "tm", 1)

    keep_low = jnp.where(row_rank == 0, 0.0, 1.0)
    keep_high = jnp.where(row_rank == row_devices - 1, 0.0, 1.0)

    def widened(block, slot):
        shape = (steps_dev, PAD, columns_dev)
        at = slice(slot * PAD, (slot + steps_dev) * PAD)
        return jnp.concatenate(
            [keep_low * low[at].reshape(shape), block, keep_high * high[at].reshape(shape)], axis=1
        )

    diff_low = jnp.where(row_rank == 0, diffusivity[:1], low[-PAD:])
    diff_high = jnp.where(row_rank == row_devices - 1, diffusivity[-1:], high[-PAD:])
    rimmed = jnp.concatenate([diff_low, diffusivity, diff_high])
    wide_iterate = widened(iterate, 0)
    faces = face_weights(jnp.pad(rimmed, ((1, 1), (0, 0)), mode="edge"))
    wide_rows = jnp.pad(wide_iterate, ((0, 0), (1, 1), (0, 0)))
    wide = time_step * (widened(forcing, steps_dev) - apply_faces(wide_rows, faces)) - wide_iterate
    wide = wide + jnp.concatenate([jnp.zeros_like(wide_iterate[:1]), wide_iterate[:-1]])
    at_row = lax.broadcasted_iota(jnp.int32, (1, rows_dev + 2 * PAD, 1), 1)
    keep = jnp.where(at_row < PAD, keep_low, jnp.where(at_row < PAD + rows_dev, 1.0, keep_high))
    wide = wide * keep
    own = wide[1:, PAD : PAD + rows_dev]
    squares_late = jnp.sum(own * own, axis=(1, 2))

    padded = rows_dev + 2 * PAD
    early = pl.pallas_call(
        functools.partial(later_steps_body, slab, halo),
        out_shape=jax.ShapeDtypeStruct(
            (time_devices, (steps_dev - 1) * tiles * rows, 128), jnp.float32
        ),
        in_specs=[smem, vmem],
        out_specs=vmem,
        compiler_params=params,
        name="later_steps",
    )(rank, wide)
    early = exchanged(early)

    previous = jnp.where(time_rank == 0, initial_state, arriving)
    before_low, before_high = border_rows((previous,), "rows", PAD)
    late, squares_first = pl.pallas_call(
        functools.partial(first_step_body, slab, halo),
        out_shape=[
            jax.ShapeDtypeStruct((time_devices, tiles * rows, 128), jnp.float32),
            jax.ShapeDtypeStruct((1, 8, 128), jnp.float32),
        ],
        in_specs=[smem] + [vmem] * 4,
        out_specs=[vmem] * 2,
        scratch_shapes=[pltpu.VMEM((padded, columns_dev), jnp.float32)],
        compiler_params=params,
        name="first_step",
    )(rank, wide, previous, before_low, before_high)
    late = lax.all_to_all(late, "tm", split_axis=0, concat_axis=0, tiled=True)

    squares = jnp.concatenate([jnp.sum(squares_first, axis=(1, 2)), squares_late])
    residual_rms = jnp.sqrt(lax.psum(squares, "rows") / cell_count + rms_eps)

    diff_slab = lax.dynamic_slice_in_dim(rimmed, slab * time_rank + PAD - halo, rows, axis=0)
    place = jnp.stack(
        [
            row_rank * rows_dev + time_rank * slab - halo,
            jnp.int32(rows_dev * row_devices),
            time_rank,
        ]
    ).astype(jnp.int32)

    vector = pltpu.VMEM((rows * length, columns_dev), jnp.float32)
    *powers, moments = pl.pallas_call(
        functools.partial(krylov_body, length, slab, halo, time_devices),
        out_shape=[vector] * DEPTH + [jax.ShapeDtypeStruct((length, 128), jnp.float32)],
        in_specs=[smem] + [vmem] * (3 + time_devices),
        out_specs=[vmem] * (DEPTH + 1),
        scratch_shapes=[
            pltpu.VMEM((time_devices, (steps_dev - 1) * tiles * rows, 128), jnp.float32),
            pltpu.VMEM((rows * 8, columns_dev), jnp.float32),
            pltpu.VMEM((rows * 8, columns_dev), jnp.float32),
            pltpu.VMEM((rows * 8, 128), jnp.float32),
        ],
        compiler_params=params,
        name="krylov",
    )(place, late, diff_slab, jnp.asarray(block_forward(length, 8)), *early)

    moments = summed_over_group(moments)

    real, imag = channel_shifts(length)
    shift = np.broadcast_to(np.stack([real, imag])[:, :, None], (2, length, 128))
    table = np.zeros((DEPTH + 1, length, 128))
    table[:, :, :MOMENTS] = power_table(length)
    corrected, doubt = pl.pallas_call(
        functools.partial(combine_body, length, slab, halo),
        out_shape=[
            jax.ShapeDtypeStruct((time_devices, steps_dev * slab, columns_dev), jnp.float32),
            jax.ShapeDtypeStruct((8, 128), jnp.float32),
        ],
        in_specs=[vmem] * (4 + DEPTH),
        out_specs=[vmem] * 2,
        compiler_params=params,
        name="combine",
    )(
        moments,
        jnp.asarray(table, jnp.float32),
        jnp.asarray(shift, jnp.float32),
        jnp.asarray(block_inverse(length, 8)),
        *powers,
    )
    back = lax.all_to_all(corrected, "tm", split_axis=0, concat_axis=0, tiled=True)

    def redone(trip, _):
        inputs = (iterate, forcing, initial_state, diffusivity)
        return careful_correction(*[jnp.where(trip < 2, value, 0.0) for value in inputs])

    back = lax.fori_loop(0, doubt[0, 0].astype(jnp.int32), redone, back)
    own_steps = back.reshape(time_devices, steps_dev, slab, columns_dev)
    own_steps = jnp.swapaxes(own_steps, 0, 1).reshape(steps_dev, rows_dev, columns_dev)
    updated = iterate + own_steps
    return (updated, residual_rms)


def solution(mesh):
    placed = (
        P(("groups", "tm"), "rows", None),
        P(("groups", "tm"), "rows", None),
        P(("groups", "rows"), None),
        P(("groups", "rows"), None),
    )
    return jax.shard_map(
        iteration,
        mesh=mesh,
        in_specs=placed,
        out_specs=(P(("groups", "tm"), "rows", None), P(("groups", "tm"))),
        check_vma=False,
    )
```

```python
import functools
import math

import jax
import jax.numpy as jnp
import numpy as np
from jax import lax
from jax.experimental import pallas as pl
from jax.experimental.pallas import tpu as pltpu
from jax.sharding import PartitionSpec as P


CG_ITERS = 3
DEPTH = 2 * CG_ITERS
MOMENTS = 2 * DEPTH + 1
UNROLL = 16
LEAST_PIVOTS = (2e-2, 2e-3)
PAD = 8

circulant_alpha = 0.05
time_step = 0.5
rms_eps = 1e-06


def from_behind(value, axis, steps):
    count = lax.axis_size(axis)
    initial, last = (max(0, -steps), min(count, count - steps))
    return lax.ppermute(value, axis, [(source, source + steps) for source in range(initial, last)])


def exchanged(pieces):
    count = pieces.shape[0]
    got = [pieces[0]] + [None] * (count - 1)
    for k in reversed(range(1, count)):
        got[k] = lax.ppermute(pieces[k], "tm", [(i, i ^ k) for i in range(count)])
    return got


def summed_over_group(values):
    for axis in ("rows", "tm"):
        count = lax.axis_size(axis)
        if count & (count - 1):
            values = lax.psum(values, axis)
        else:
            step = 1
            while step < count:
                pairs = [(i, i ^ step) for i in range(count)]
                values = values + lax.ppermute(values, axis, pairs)
                step *= 2
    return values


def extended(block, axis, dim, width):
    count = lax.axis_size(axis)
    forward = [(i, i + 1) for i in range(count - 1)]
    backward = [(target, source) for source, target in forward]
    low = lax.slice_in_dim(block, block.shape[dim] - width, None, axis=dim)
    high = lax.slice_in_dim(block, 0, width, axis=dim)
    low, high = lax.ppermute(low, axis, forward), lax.ppermute(high, axis, backward)
    return jnp.concatenate([low, block, high], axis=dim)


def finish_body(slab, iterate_ref, back_ref, out_ref, got_ref, sum_ref, arrived, left):
    chunks = back_ref.shape[0]
    copies = [
        pltpu.make_async_copy(back_ref.at[k], got_ref.at[k], arrived.at[k]) for k in range(chunks)
    ]
    for copy in copies:
        copy.start()
    leaving = []
    for k in range(chunks):
        copies[k].wait()
        at = slice(slab * k, slab * (k + 1))
        for s in range(iterate_ref.shape[0]):
            sum_ref[s, at, :] = iterate_ref[s, at, :] + got_ref[k, slab * s : slab * (s + 1), :]
        leaving.append(
            pltpu.make_async_copy(sum_ref.at[:, at, :], out_ref.at[:, at, :], left.at[k])
        )
        leaving[-1].start()
    for copy in leaving:
        copy.wait()


def careful_correction(iterate, forcing, initial_state, diffusivity):
    steps_dev, rows_dev, columns = iterate.shape
    time_devices = lax.axis_size("tm")
    row_devices = lax.axis_size("rows")
    time_rank = lax.axis_index("tm")
    row_rank = lax.axis_index("rows")
    length = steps_dev * time_devices
    half = length // 2
    slab = rows_dev // time_devices
    halo = -(-(DEPTH + 1) // 8) * 8
    rows = slab + 2 * halo
    rimmed = extended(diffusivity, "rows", 0, halo)
    at = lax.broadcasted_iota(jnp.int32, (rows_dev + 2 * halo, 1), 0)
    rimmed = jnp.where((row_rank == 0) & (at < halo), diffusivity[:1], rimmed)
    beyond = (row_rank == row_devices - 1) & (at >= halo + rows_dev)
    rimmed = jnp.where(beyond, diffusivity[-1:], rimmed)
    arriving = from_behind(iterate[-1], "tm", 1)
    first_previous = jnp.where(time_rank == 0, initial_state, arriving)
    previous = jnp.concatenate([first_previous[None], iterate[:-1]], axis=0)
    faces = face_weights(rimmed[halo - 1 : halo + rows_dev + 1])
    spread = apply_faces(extended(iterate, "rows", 1, 1), faces)
    residual = time_step * forcing + previous - iterate - time_step * spread
    wide = extended(residual, "rows", 1, halo)
    pieces = jnp.stack(
        [lax.slice_in_dim(wide, slab * k, slab * k + rows, axis=1) for k in range(time_devices)]
    )
    pieces = lax.all_to_all(pieces, "tm", split_axis=0, concat_axis=0, tiled=True)
    flat = pieces.reshape(length, rows * columns)
    spectrum = jnp.dot(
        jnp.asarray(forward_matrix(length), jnp.float32), flat, precision=lax.Precision.HIGHEST
    ).reshape(length, rows, columns)

    slab_faces = face_weights(
        jnp.pad(
            lax.dynamic_slice_in_dim(rimmed, slab * time_rank, rows, axis=0),
            ((1, 1), (0, 0)),
            mode="edge",
        )
    )
    place = lax.broadcasted_iota(jnp.int32, (1, rows, 1), 1) - halo
    grid_row = place + row_rank * rows_dev + time_rank * slab
    inside = (grid_row >= 0) & (grid_row < rows_dev * row_devices)
    own = (place >= 0) & (place < slab)
    real, imag = channel_shifts(length)
    real = jnp.asarray(real[:, None, None], jnp.float32)
    imag = jnp.asarray(imag[:, None, None], jnp.float32)
    channel = lax.broadcasted_iota(jnp.int32, (length, 1, 1), 0)
    alone = (channel == 0) | (channel == half)

    def operate(values, orientation):
        padded = jnp.pad(values, ((0, 0), (1, 1), (0, 0)))
        spread = time_step * apply_faces(padded, slab_faces)
        swapped = jnp.concatenate([-values[half:], values[:half]])
        return jnp.where(inside, real * values + orientation * imag * swapped + spread, 0.0)

    def norm(values):
        sums = jnp.sum(jnp.where(own, values * values, 0.0), axis=(1, 2), keepdims=True)
        sums = summed_over_group(sums)
        return jnp.where(alone, sums, sums + jnp.concatenate([sums[half:], sums[:half]]))

    def iterated(_, state):
        result, remain, search, gamma = state
        image = operate(search, 1.0)
        rate = gamma / norm(image)
        result = result + rate * search
        remain = remain - rate * image
        normal = operate(remain, -1.0)
        gamma_next = norm(normal)
        search = normal + (gamma_next / gamma) * search
        return result, remain, search, gamma_next

    normal = operate(spectrum, -1.0)
    state = (jnp.zeros_like(spectrum), spectrum, normal, norm(normal))
    result = lax.fori_loop(0, CG_ITERS, iterated, state)[0]
    result = result[:, halo : halo + slab].reshape(length, slab * columns)
    corrected = jnp.dot(
        jnp.asarray(inverse_matrix(length), jnp.float32), result, precision=lax.Precision.HIGHEST
    ).reshape(time_devices, steps_dev * slab, columns)
    return lax.all_to_all(corrected, "tm", split_axis=0, concat_axis=0, tiled=True)


def border_rows(blocks, axis, width):
    count = lax.axis_size(axis)
    if count == 2:
        first = lax.axis_index(axis) == 0

        def edge(block):
            return jnp.where(first, block[..., -width:, :], block[..., :width, :])

        mine = jnp.concatenate([edge(block).reshape(-1, block.shape[-1]) for block in blocks])
        got = lax.ppermute(mine, axis, [(0, 1), (1, 0)])
        return got, got
    low = jnp.concatenate([b[..., -width:, :].reshape(-1, b.shape[-1]) for b in blocks])
    high = jnp.concatenate([b[..., :width, :].reshape(-1, b.shape[-1]) for b in blocks])
    return (
        lax.ppermute(low, axis, [(i, i + 1) for i in range(count - 1)]),
        lax.ppermute(high, axis, [(i + 1, i) for i in range(count - 1)]),
    )


def growth_of(length):
    return np.exp(math.log(circulant_alpha) * np.arange(length) / length)


def forward_matrix(length):
    half = length // 2
    steps = np.arange(length)
    table = np.zeros((length, length))
    for j in range(half):
        turn = 2 * np.pi * ((j * steps) % length) / length
        table[j] = np.cos(turn)
        table[half + j] = -np.sin(turn)
    table[half] = np.cos(2 * np.pi * ((half * steps) % length) / length)
    return table * growth_of(length)[None, :]


def inverse_matrix(length):
    half = length // 2
    steps = np.arange(length)
    table = np.zeros((length, length))
    for j in range(half):
        turn = 2 * np.pi * ((j * steps) % length) / length
        weight = 1.0 if j == 0 else 2.0
        table[:, j] = weight * np.cos(turn) / length
        table[:, half + j] = -weight * np.sin(turn) / length
    table[:, half] = np.cos(2 * np.pi * ((half * steps) % length) / length) / length
    return table / growth_of(length)[:, None]


def block_forward(length, rows):
    full = np.einsum("cn,rs->rcns", forward_matrix(length), np.eye(rows))
    return full.reshape(rows * length, length * rows).astype(np.float32)


def block_inverse(length, rows):
    full = np.einsum("nc,rs->nrsc", inverse_matrix(length), np.eye(rows))
    return full.reshape(length * rows, rows * length).astype(np.float32)


def channel_shifts(length):
    half = length // 2
    root = math.exp(math.log(circulant_alpha) / length)
    freq = np.concatenate([np.arange(half), np.arange(half)])
    freq[half] = half
    angle = 2 * np.pi * freq / length
    real = 1 - root * np.cos(angle)
    imag = root * np.sin(angle)
    imag[0] = 0.0
    imag[half] = 0.0
    return real, imag


def power_table(length):
    real, imag = channel_shifts(length)
    base = np.stack([real**2 + imag**2, 2 * real, np.ones_like(real)], axis=1)
    powers = [np.concatenate([np.ones((length, 1)), np.zeros((length, MOMENTS - 1))], axis=1)]
    for _ in range(DEPTH):
        last = powers[-1]
        following = np.zeros_like(last)
        for m in range(3):
            following[:, m:] += base[:, m : m + 1] * last[:, : MOMENTS - m]
        powers.append(following)
    return np.stack(powers)


def face_weights(padded_rows):
    centre = padded_rows[1:-1]
    columns = jnp.pad(centre, ((0, 0), (1, 1)), mode="edge")
    return (
        0.5 * (centre + padded_rows[:-2]),
        0.5 * (centre + padded_rows[2:]),
        0.5 * (centre + columns[:, :-2]),
        0.5 * (centre + columns[:, 2:]),
    )


def apply_faces(padded_rows, weights):
    north, south, west, east = weights
    centre = padded_rows[..., 1:-1, :]
    columns = jnp.pad(centre, [(0, 0)] * (centre.ndim - 1) + [(1, 1)])
    return (
        (north + south + west + east) * centre
        - north * padded_rows[..., :-2, :]
        - south * padded_rows[..., 2:, :]
        - west * columns[..., :-2]
        - east * columns[..., 2:]
    )


def borders_body(iterate_ref, forcing_ref, diff_ref, mine_ref, last_ref, rim_ref, done):
    steps, rows_dev, _ = iterate_ref.shape
    start = pl.multiple_of(jnp.where(lax.axis_index("rows") == 0, rows_dev - PAD, 0), 8)
    copies = []
    for s in range(steps):
        copies.append((iterate_ref.at[s, pl.ds(start, PAD)], mine_ref.at[pl.ds(PAD * s, PAD)]))
        at = PAD * (steps + s)
        copies.append((forcing_ref.at[s, pl.ds(start, PAD)], mine_ref.at[pl.ds(at, PAD)]))
    copies.append((diff_ref.at[pl.ds(start, PAD)], mine_ref.at[pl.ds(2 * PAD * steps, PAD)]))
    copies.append((diff_ref.at[pl.ds(0, PAD)], rim_ref.at[pl.ds(0, PAD)]))
    copies.append((diff_ref.at[pl.ds(rows_dev - PAD, PAD)], rim_ref.at[pl.ds(PAD, PAD)]))
    copies.append((iterate_ref.at[steps - 1], last_ref))
    started = []
    for index, (source, target) in enumerate(copies):
        started.append(pltpu.make_async_copy(source, target, done.at[index]))
        started[-1].start()
    for copy in started:
        copy.wait()


def pack(out_ref, at, source_ref, slab, halo, flip=0):
    rows = slab + 2 * halo
    for target in range(out_ref.shape[0]):
        first = slab * target + PAD - halo
        for t in range(source_ref.shape[-1] // 128):
            out_ref[target ^ flip, at + rows * t : at + rows * (t + 1), :] = source_ref[
                first : first + rows, 128 * t : 128 * (t + 1)
            ]


def later_steps_body(slab, halo, wide_ref, pieces_ref):
    steps, _, columns = wide_ref.shape
    for s in range(1, steps):
        at = (s - 1) * (columns // 128) * (slab + 2 * halo)
        pack(pieces_ref, at, wide_ref.at[s], slab, halo)


def first_step_body(slab, halo, rank_ref, partial_ref, previous_ref, low_ref, high_ref,
                    pieces_ref, squares_ref, whole_ref):
    rows_dev, columns = previous_ref.shape
    keep_low = jnp.where(rank_ref[0] == 0, 0.0, 1.0)
    keep_high = jnp.where(rank_ref[0] == rank_ref[1] - 1, 0.0, 1.0)
    whole_ref[:PAD, :] = partial_ref[0, :PAD, :] + keep_low * low_ref[...]
    whole_ref[PAD + rows_dev :, :] = partial_ref[0, PAD + rows_dev :, :] + keep_high * high_ref[...]
    squares = jnp.zeros((8, columns), jnp.float32)
    for at in range(0, rows_dev, 8):
        value = partial_ref[0, PAD + at : PAD + at + 8, :] + previous_ref[at : at + 8, :]
        whole_ref[PAD + at : PAD + at + 8, :] = value
        squares = squares + value * value
    total = squares[:, :128]
    for t in range(1, columns // 128):
        total = total + squares[:, 128 * t : 128 * t + 128]
    squares_ref[0] = total
    pack(pieces_ref, 0, whole_ref, slab, halo, rank_ref[2])


def put_weights(diff_ref, south_ref, east_ref, west_ref):
    rows, columns = diff_ref.shape
    centre = diff_ref[...]
    below = jnp.concatenate([centre[1:], centre[-1:]], axis=0)
    lane = lax.broadcasted_iota(jnp.int32, (rows, columns), 1)
    after = jnp.where(lane == columns - 1, centre, pltpu.roll(centre, columns - 1, 1))
    quarter = 0.5 * time_step
    south = quarter * (centre + below)
    east = quarter * (centre + after)
    west = (2.0 * quarter) * centre[:, :128]
    for r in range(rows):
        south_ref[8 * r : 8 * r + 8, :] = jnp.broadcast_to(south[r : r + 1], (8, columns))
        east_ref[8 * r : 8 * r + 8, :] = jnp.broadcast_to(east[r : r + 1], (8, columns))
        west_ref[8 * r : 8 * r + 8, :] = jnp.broadcast_to(west[r : r + 1], (8, 128))


def transform(target, early_ref, late_ref, mix, rows, length, tiles):
    sources = early_ref.shape[0]
    steps_dev = length // sources
    starts = list(range(0, rows - 7, 8))
    if starts[-1] + 8 < rows:
        starts.append(rows - 8)
    for start in starts:
        for t in range(tiles):
            cells = []
            for source in range(sources):
                for step in range(steps_dev):
                    ref = late_ref if step == 0 else early_ref
                    at = (max(step - 1, 0) * tiles + t) * rows + start
                    cells.append(ref[source, at : at + 8, :])
            target[start * length : (start + 8) * length, 128 * t : 128 * t + 128] = jnp.dot(
                mix,
                jnp.concatenate(cells, axis=0),
                precision=lax.Precision.HIGH,
                preferred_element_type=jnp.float32,
            )


def krylov_body(length, slab, halo, sources, place_ref, early_ref, diff_ref, mix_ref, *rest):
    pieces = rest[:sources]
    vectors = rest[sources : sources + DEPTH]
    moments_ref, late_ref, south_ref, east_ref, west_ref = rest[sources + DEPTH :]
    rows = slab + 2 * halo
    columns = diff_ref.shape[-1]
    groups = length // 8
    tiles = columns // 128
    first_row = place_ref[0] + halo == 0
    last_row = place_ref[0] + halo + slab == place_ref[1]
    keep_above = jnp.where(first_row, 0.0, 1.0)
    keep_below = jnp.where(last_row, 0.0, 1.0)
    put_weights(diff_ref, south_ref, east_ref, west_ref)
    for index, piece in enumerate(pieces):
        late_ref[index ^ place_ref[2]] = piece[...]
    transform(vectors[0], early_ref, late_ref, mix_ref[...], rows, length, tiles)

    lane8 = lax.broadcasted_iota(jnp.int32, (8, 128), 1)
    is_first = lane8 == 0
    is_last = lane8 == 127

    def load(source, r, group):
        at = pl.multiple_of(r * length + 8 * group, 8)
        return [source[pl.ds(at, 8), 128 * t : 128 * t + 128] for t in range(tiles)]

    def row_of(ref, r, t):
        return ref[pl.ds(pl.multiple_of(8 * r, 8), 8), 128 * t : 128 * t + 128]

    def south_flux(r, here, under):
        return [row_of(south_ref, r, t) * (under[t] - here[t]) for t in range(tiles)]

    def stencil(r, here, under, north):
        south = south_flux(r, here, under)
        turned = [pltpu.roll(v, 127, 1) for v in here] + [0.0]
        east = [
            row_of(east_ref, r, t) * (jnp.where(is_last, turned[t + 1], turned[t]) - here[t])
            for t in range(tiles)
        ]
        moved = [row_of(west_ref, r, 0) * here[0]] + [pltpu.roll(f, 1, 1) for f in east]
        value = [
            (jnp.where(is_first, moved[t], moved[t + 1]) - east[t]) + (north[t] - south[t])
            for t in range(tiles)
        ]
        return value, south

    def total(parts):
        while len(parts) > 1:
            parts = [parts[i] + parts[i + 1] for i in range(0, len(parts) - 1, 2)] + (
                [parts[-1]] if len(parts) % 2 else []
            )
        return parts[0]

    table = [jnp.zeros((8, 128), jnp.float32) for _ in range(groups)]

    def put(entry, index, sums):
        return jnp.where(lane8 == index, jnp.sum(sums, axis=1, keepdims=True), entry)

    for power in range(DEPTH):
        source = vectors[power]
        target = vectors[power + 1] if power + 1 < DEPTH else None
        first, final = power + 1, rows - 1 - power
        for group in range(groups):

            def step(r, carry, summing):
                here, north, sums = carry
                under = load(source, r + 1, group)
                value, south = stencil(r, here, under, north)
                if target is not None:
                    at = pl.multiple_of(r * length + 8 * group, 8)
                    for t in range(tiles):
                        target[pl.ds(at, 8), 128 * t : 128 * t + 128] = value[t]
                if summing:
                    products = [
                        sums[0] + total([v * v for v in here]),
                        sums[1] + total([v * w for v, w in zip(here, value)]),
                    ]
                    if target is None:
                        products.append(sums[2] + total([w * w for w in value]))
                    sums = tuple(products)
                return tuple(under), tuple(south), sums

            top = load(source, first - 1, group)
            here = load(source, first, group)
            carry = (tuple(here), tuple(south_flux(first - 1, top, here)), ())
            if first < halo:
                carry = lax.fori_loop(
                    first, halo, functools.partial(step, summing=False), carry, unroll=True
                )
            zero = jnp.zeros((8, 128), jnp.float32)
            carry = (carry[0], carry[1], (zero,) * (2 if target is not None else 3))
            carry = lax.fori_loop(
                halo, halo + slab, functools.partial(step, summing=True), carry, unroll=min(UNROLL, max(1, slab // 2))
            )
            for index, sums in enumerate(carry[2]):
                table[group] = put(table[group], 2 * power + index, sums)
            if first < halo:
                carry = (carry[0], carry[1], ())
                lax.fori_loop(
                    halo + slab, final, functools.partial(step, summing=False), carry, unroll=True
                )
            if target is not None and first < halo:
                for r, keep in ((halo - 1, keep_above), (halo + slab, keep_below)):
                    at = r * length + 8 * group
                    target[at : at + 8, :] = target[at : at + 8, :] * keep
    moments_ref[...] = jnp.concatenate(table, axis=0)


def combine_body(length, slab, halo, moments_ref, table_ref, shift_ref, mix_ref, *rest):
    power_refs = rest[:DEPTH]
    out_ref, doubt_ref = rest[DEPTH:]
    steps_dev = out_ref.shape[1] // slab
    half = length // 2
    own = moments_ref[...]
    swapped = jnp.concatenate([own[half:], own[:half]], axis=0)
    channel = lax.broadcasted_iota(jnp.int32, own.shape, 0)
    alone = (channel == 0) | (channel == half)
    sums = jnp.where(alone, own, own + swapped)
    mu = [
        jnp.sum(sums * table_ref[k + 1], axis=1, keepdims=True) for k in range(2 * CG_ITERS)
    ]
    low1, low2 = mu[2] / mu[1], mu[3] / mu[1]
    pivot1 = mu[3] - low1 * mu[2]
    cross = mu[4] - low1 * mu[3]
    pivot2 = mu[5] - low2 * mu[3]
    right1 = mu[1] - low1 * mu[0]
    right2 = mu[2] - low2 * mu[0]
    low3 = cross / pivot1
    pivot2 = pivot2 - low3 * cross
    right2 = right2 - low3 * right1
    sound = (pivot1 > LEAST_PIVOTS[0] * mu[3]) & (pivot2 > LEAST_PIVOTS[1] * mu[5])
    doubt = jnp.max(jnp.where(sound, 0.0, 1.0), axis=0, keepdims=True)
    doubt_ref[...] = jnp.broadcast_to(doubt, doubt_ref.shape)
    c2 = right2 / pivot2
    c1 = (right1 - cross * c2) / pivot1
    c0 = (mu[0] - mu[2] * c1 - mu[3] * c2) / mu[1]
    inner = c0 * table_ref[0] + c1 * table_ref[1] + c2 * table_ref[2]
    real = shift_ref[0]
    imag = shift_ref[1]
    lanes = lax.broadcasted_iota(jnp.int32, inner.shape, 1)
    outer = real * inner + jnp.where(lanes == 0, 0.0, pltpu.roll(inner, 1, 1))
    crossed = imag * inner
    sign = jnp.where(lax.broadcasted_iota(jnp.int32, inner.shape, 0) < half, 1.0, -1.0)
    crossed = sign * crossed
    columns = out_ref.shape[-1]

    def spread(values, index):
        return jnp.broadcast_to(values[:, index : index + 1], (length, columns))[None]

    for start in range(0, slab, 8):
        total = jnp.zeros((8, length, columns), jnp.float32)
        other = jnp.zeros((8, length, columns), jnp.float32)
        for power in range(DEPTH):
            at = (halo + start) * length
            here = power_refs[power][at : at + 8 * length, :].reshape(8, length, columns)
            total = total + spread(outer, power) * here
            if power + 1 < DEPTH:
                flipped = jnp.concatenate([here[:, half:], here[:, :half]], axis=1)
                other = other + spread(crossed, power) * flipped
        block = (total + other).reshape(8 * length, columns)
        result = jnp.dot(
            mix_ref[...], block, precision=lax.Precision.HIGH, preferred_element_type=jnp.float32
        )
        for step in range(length):
            at = (step % steps_dev) * slab + start
            out_ref[step // steps_dev, at : at + 8, :] = result[step * 8 : step * 8 + 8]


def iteration(iterate, forcing, initial_state, diffusivity):
    steps_dev, rows_dev, columns_dev = iterate.shape
    time_devices = lax.axis_size("tm")
    row_devices = lax.axis_size("rows")
    time_rank = lax.axis_index("tm")
    row_rank = lax.axis_index("rows")
    length = steps_dev * time_devices
    cell_count = rows_dev * row_devices * columns_dev
    slab = rows_dev // time_devices
    halo = DEPTH
    rows = slab + 2 * halo

    tiles = columns_dev // 128
    vmem = pl.BlockSpec(memory_space=pltpu.VMEM)
    smem = pl.BlockSpec(memory_space=pltpu.SMEM)
    params = pltpu.CompilerParams(vmem_limit_bytes=24 * 2**20)
    rank = jnp.stack([row_rank, jnp.int32(row_devices), time_rank]).astype(jnp.int32)

    if row_devices == 2:
        mine, last, rim = pl.pallas_call(
            borders_body,
            out_shape=[
                pltpu.VMEM(((2 * steps_dev + 1) * PAD, columns_dev), jnp.float32),
                pltpu.VMEM((rows_dev, columns_dev), jnp.float32),
                pltpu.VMEM((2 * PAD, columns_dev), jnp.float32),
            ],
            in_specs=[pl.BlockSpec(memory_space=pltpu.HBM)] * 3,
            out_specs=[vmem] * 3,
            scratch_shapes=[pltpu.SemaphoreType.DMA((2 * steps_dev + 4,))],
            compiler_params=pltpu.CompilerParams(vmem_limit_bytes=2**26 - 3 * 2**18),
            name="borders",
        )(iterate, forcing, diffusivity)
        low = high = lax.ppermute(mine, "rows", [(0, 1), (1, 0)])
    else:
        last = iterate[-1]
        rim = jnp.concatenate([diffusivity[:PAD], diffusivity[-PAD:]])
        low, high = border_rows((iterate, forcing, diffusivity), "rows", PAD)
    arriving = from_behind(last, "tm", 1)

    keep_low = jnp.where(row_rank == 0, 0.0, 1.0)
    keep_high = jnp.where(row_rank == row_devices - 1, 0.0, 1.0)

    def widened(block, slot):
        shape = (steps_dev, PAD, columns_dev)
        at = slice(slot * PAD, (slot + steps_dev) * PAD)
        return jnp.concatenate(
            [keep_low * low[at].reshape(shape), block, keep_high * high[at].reshape(shape)], axis=1
        )

    diff_low = jnp.where(row_rank == 0, rim[:1], low[-PAD:])
    diff_high = jnp.where(row_rank == row_devices - 1, rim[-1:], high[-PAD:])
    rimmed = jnp.concatenate([diff_low, diffusivity, diff_high])
    wide_iterate = widened(iterate, 0)
    faces = face_weights(jnp.pad(rimmed, ((1, 1), (0, 0)), mode="edge"))
    wide_rows = jnp.pad(wide_iterate, ((0, 0), (1, 1), (0, 0)))
    wide = time_step * (widened(forcing, steps_dev) - apply_faces(wide_rows, faces)) - wide_iterate
    wide = wide + jnp.concatenate([jnp.zeros_like(wide_iterate[:1]), wide_iterate[:-1]])
    at_row = lax.broadcasted_iota(jnp.int32, (1, rows_dev + 2 * PAD, 1), 1)
    keep = jnp.where(at_row < PAD, keep_low, jnp.where(at_row < PAD + rows_dev, 1.0, keep_high))
    wide = wide * keep
    own = wide[1:, PAD : PAD + rows_dev]
    squares_late = jnp.sum(own * own, axis=(1, 2))

    padded = rows_dev + 2 * PAD
    early = pl.pallas_call(
        functools.partial(later_steps_body, slab, halo),
        out_shape=jax.ShapeDtypeStruct(
            (time_devices, (steps_dev - 1) * tiles * rows, 128), jnp.float32
        ),
        in_specs=[vmem],
        out_specs=vmem,
        compiler_params=params,
        name="later_steps",
    )(wide)
    early = lax.all_to_all(early, "tm", split_axis=0, concat_axis=0, tiled=True)

    previous = jnp.where(time_rank == 0, initial_state, arriving)
    before_low, before_high = border_rows((previous,), "rows", PAD)
    late, squares_first = pl.pallas_call(
        functools.partial(first_step_body, slab, halo),
        out_shape=[
            jax.ShapeDtypeStruct((time_devices, tiles * rows, 128), jnp.float32),
            jax.ShapeDtypeStruct((1, 8, 128), jnp.float32),
        ],
        in_specs=[smem] + [vmem] * 4,
        out_specs=[vmem] * 2,
        scratch_shapes=[pltpu.VMEM((padded, columns_dev), jnp.float32)],
        compiler_params=params,
        name="first_step",
    )(rank, wide, previous, before_low, before_high)
    late = exchanged(late)

    squares = jnp.concatenate([jnp.sum(squares_first, axis=(1, 2)), squares_late])
    residual_rms = jnp.sqrt(lax.psum(squares, "rows") / cell_count + rms_eps)

    diff_slab = lax.dynamic_slice_in_dim(rimmed, slab * time_rank + PAD - halo, rows, axis=0)
    place = jnp.stack(
        [
            row_rank * rows_dev + time_rank * slab - halo,
            jnp.int32(rows_dev * row_devices),
            time_rank,
        ]
    ).astype(jnp.int32)

    vector = pltpu.VMEM((rows * length, columns_dev), jnp.float32)
    *powers, moments = pl.pallas_call(
        functools.partial(krylov_body, length, slab, halo, time_devices),
        out_shape=[vector] * DEPTH + [jax.ShapeDtypeStruct((length, 128), jnp.float32)],
        in_specs=[smem] + [vmem] * (3 + time_devices),
        out_specs=[vmem] * (DEPTH + 1),
        scratch_shapes=[
            pltpu.VMEM((time_devices, tiles * rows, 128), jnp.float32),
            pltpu.VMEM((rows * 8, columns_dev), jnp.float32),
            pltpu.VMEM((rows * 8, columns_dev), jnp.float32),
            pltpu.VMEM((rows * 8, 128), jnp.float32),
        ],
        compiler_params=params,
        name="krylov",
    )(place, early, diff_slab, jnp.asarray(block_forward(length, 8)), *late)

    moments = summed_over_group(moments)

    real, imag = channel_shifts(length)
    shift = np.broadcast_to(np.stack([real, imag])[:, :, None], (2, length, 128))
    table = np.zeros((DEPTH + 1, length, 128))
    table[:, :, :MOMENTS] = power_table(length)
    corrected, doubt = pl.pallas_call(
        functools.partial(combine_body, length, slab, halo),
        out_shape=[
            jax.ShapeDtypeStruct((time_devices, steps_dev * slab, columns_dev), jnp.float32),
            jax.ShapeDtypeStruct((8, 128), jnp.float32),
        ],
        in_specs=[vmem] * (4 + DEPTH),
        out_specs=[vmem] * 2,
        compiler_params=params,
        name="combine",
    )(
        moments,
        jnp.asarray(table, jnp.float32),
        jnp.asarray(shift, jnp.float32),
        jnp.asarray(block_inverse(length, 8)),
        *powers,
    )
    back = lax.all_to_all(corrected, "tm", split_axis=0, concat_axis=0, tiled=True)

    def redone(trip, _):
        inputs = (iterate, forcing, initial_state, diffusivity)
        return careful_correction(*[jnp.where(trip < 2, value, 0.0) for value in inputs])

    back = lax.fori_loop(0, doubt[0, 0].astype(jnp.int32), redone, back)
    updated = pl.pallas_call(
        functools.partial(finish_body, slab),
        out_shape=jax.ShapeDtypeStruct(iterate.shape, jnp.float32),
        in_specs=[vmem, pl.BlockSpec(memory_space=pl.ANY)],
        out_specs=pl.BlockSpec(memory_space=pltpu.HBM),
        scratch_shapes=[
            pltpu.VMEM(back.shape, jnp.float32),
            pltpu.VMEM(iterate.shape, jnp.float32),
            pltpu.SemaphoreType.DMA((time_devices,)),
            pltpu.SemaphoreType.DMA((time_devices,)),
        ],
        compiler_params=params,
        name="finish",
    )(iterate, back)
    return (updated, residual_rms)


def solution(mesh):
    placed = (
        P(("groups", "tm"), "rows", None),
        P(("groups", "tm"), "rows", None),
        P(("groups", "rows"), None),
        P(("groups", "rows"), None),
    )
    return jax.shard_map(
        iteration,
        mesh=mesh,
        in_specs=placed,
        out_specs=(P(("groups", "tm"), "rows", None), P(("groups", "tm"))),
        check_vma=False,
    )
```

```python
import functools
import math

import jax
import jax.numpy as jnp
import numpy as np
from jax import lax
from jax.experimental import pallas as pl
from jax.experimental.pallas import tpu as pltpu
from jax.sharding import PartitionSpec as P


CG_ITERS = 3
DEPTH = 2 * CG_ITERS
MOMENTS = 2 * DEPTH + 1
UNROLL = 16
LEAST_PIVOTS = (8e-2, 8e-3)
PAD = 8

circulant_alpha = 0.05
time_step = 0.5
rms_eps = 1e-06


def from_behind(value, axis, steps):
    count = lax.axis_size(axis)
    initial, last = (max(0, -steps), min(count, count - steps))
    return lax.ppermute(value, axis, [(source, source + steps) for source in range(initial, last)])


def exchanged(pieces):
    count = pieces.shape[0]
    got = [pieces[0]] + [None] * (count - 1)
    for k in reversed(range(1, count)):
        got[k] = lax.ppermute(pieces[k], "tm", [(i, i ^ k) for i in range(count)])
    return got


def summed_over_group(values):
    for axis in ("rows", "tm"):
        count = lax.axis_size(axis)
        if count & (count - 1):
            values = lax.psum(values, axis)
        else:
            step = 1
            while step < count:
                pairs = [(i, i ^ step) for i in range(count)]
                values = values + lax.ppermute(values, axis, pairs)
                step *= 2
    return values


def extended(block, axis, dim, width):
    count = lax.axis_size(axis)
    forward = [(i, i + 1) for i in range(count - 1)]
    backward = [(target, source) for source, target in forward]
    low = lax.slice_in_dim(block, block.shape[dim] - width, None, axis=dim)
    high = lax.slice_in_dim(block, 0, width, axis=dim)
    low, high = lax.ppermute(low, axis, forward), lax.ppermute(high, axis, backward)
    return jnp.concatenate([low, block, high], axis=dim)


def finish_body(slab, iterate_ref, back_ref, out_ref, got_ref, sum_ref, arrived, left):
    chunks = back_ref.shape[0]
    copies = [
        pltpu.make_async_copy(back_ref.at[k], got_ref.at[k], arrived.at[k]) for k in range(chunks)
    ]
    for copy in copies:
        copy.start()
    leaving = []
    for k in range(chunks):
        copies[k].wait()
        at = slice(slab * k, slab * (k + 1))
        for s in range(iterate_ref.shape[0]):
            sum_ref[s, at, :] = iterate_ref[s, at, :] + got_ref[k, slab * s : slab * (s + 1), :]
        leaving.append(
            pltpu.make_async_copy(sum_ref.at[:, at, :], out_ref.at[:, at, :], left.at[k])
        )
        leaving[-1].start()
    for copy in leaving:
        copy.wait()


def careful_correction(iterate, forcing, initial_state, diffusivity):
    steps_dev, rows_dev, columns = iterate.shape
    time_devices = lax.axis_size("tm")
    row_devices = lax.axis_size("rows")
    time_rank = lax.axis_index("tm")
    row_rank = lax.axis_index("rows")
    length = steps_dev * time_devices
    half = length // 2
    slab = rows_dev // time_devices
    halo = -(-(DEPTH + 1) // 8) * 8
    rows = slab + 2 * halo
    rimmed = extended(diffusivity, "rows", 0, halo)
    at = lax.broadcasted_iota(jnp.int32, (rows_dev + 2 * halo, 1), 0)
    rimmed = jnp.where((row_rank == 0) & (at < halo), diffusivity[:1], rimmed)
    beyond = (row_rank == row_devices - 1) & (at >= halo + rows_dev)
    rimmed = jnp.where(beyond, diffusivity[-1:], rimmed)
    arriving = from_behind(iterate[-1], "tm", 1)
    first_previous = jnp.where(time_rank == 0, initial_state, arriving)
    previous = jnp.concatenate([first_previous[None], iterate[:-1]], axis=0)
    faces = face_weights(rimmed[halo - 1 : halo + rows_dev + 1])
    spread = apply_faces(extended(iterate, "rows", 1, 1), faces)
    residual = time_step * forcing + previous - iterate - time_step * spread
    wide = extended(residual, "rows", 1, halo)
    pieces = jnp.stack(
        [lax.slice_in_dim(wide, slab * k, slab * k + rows, axis=1) for k in range(time_devices)]
    )
    pieces = lax.all_to_all(pieces, "tm", split_axis=0, concat_axis=0, tiled=True)
    flat = pieces.reshape(length, rows * columns)
    spectrum = jnp.dot(
        jnp.asarray(forward_matrix(length), jnp.float32), flat, precision=lax.Precision.HIGHEST
    ).reshape(length, rows, columns)

    slab_faces = face_weights(
        jnp.pad(
            lax.dynamic_slice_in_dim(rimmed, slab * time_rank, rows, axis=0),
            ((1, 1), (0, 0)),
            mode="edge",
        )
    )
    place = lax.broadcasted_iota(jnp.int32, (1, rows, 1), 1) - halo
    grid_row = place + row_rank * rows_dev + time_rank * slab
    inside = (grid_row >= 0) & (grid_row < rows_dev * row_devices)
    own = (place >= 0) & (place < slab)
    real, imag = channel_shifts(length)
    real = jnp.asarray(real[:, None, None], jnp.float32)
    imag = jnp.asarray(imag[:, None, None], jnp.float32)
    channel = lax.broadcasted_iota(jnp.int32, (length, 1, 1), 0)
    alone = (channel == 0) | (channel == half)

    def operate(values, orientation):
        padded = jnp.pad(values, ((0, 0), (1, 1), (0, 0)))
        spread = time_step * apply_faces(padded, slab_faces)
        swapped = jnp.concatenate([-values[half:], values[:half]])
        return jnp.where(inside, real * values + orientation * imag * swapped + spread, 0.0)

    def norm(values):
        sums = jnp.sum(jnp.where(own, values * values, 0.0), axis=(1, 2), keepdims=True)
        sums = summed_over_group(sums)
        return jnp.where(alone, sums, sums + jnp.concatenate([sums[half:], sums[:half]]))

    def iterated(_, state):
        result, remain, search, gamma = state
        image = operate(search, 1.0)
        rate = gamma / norm(image)
        result = result + rate * search
        remain = remain - rate * image
        normal = operate(remain, -1.0)
        gamma_next = norm(normal)
        search = normal + (gamma_next / gamma) * search
        return result, remain, search, gamma_next

    normal = operate(spectrum, -1.0)
    state = (jnp.zeros_like(spectrum), spectrum, normal, norm(normal))
    result = lax.fori_loop(0, CG_ITERS, iterated, state)[0]
    result = result[:, halo : halo + slab].reshape(length, slab * columns)
    corrected = jnp.dot(
        jnp.asarray(inverse_matrix(length), jnp.float32), result, precision=lax.Precision.HIGHEST
    ).reshape(time_devices, steps_dev * slab, columns)
    return lax.all_to_all(corrected, "tm", split_axis=0, concat_axis=0, tiled=True)


def border_rows(blocks, axis, width):
    count = lax.axis_size(axis)
    if count == 2:
        first = lax.axis_index(axis) == 0

        def edge(block):
            return jnp.where(first, block[..., -width:, :], block[..., :width, :])

        mine = jnp.concatenate([edge(block).reshape(-1, block.shape[-1]) for block in blocks])
        got = lax.ppermute(mine, axis, [(0, 1), (1, 0)])
        return got, got
    low = jnp.concatenate([b[..., -width:, :].reshape(-1, b.shape[-1]) for b in blocks])
    high = jnp.concatenate([b[..., :width, :].reshape(-1, b.shape[-1]) for b in blocks])
    return (
        lax.ppermute(low, axis, [(i, i + 1) for i in range(count - 1)]),
        lax.ppermute(high, axis, [(i + 1, i) for i in range(count - 1)]),
    )


def growth_of(length):
    return np.exp(math.log(circulant_alpha) * np.arange(length) / length)


def forward_matrix(length):
    half = length // 2
    steps = np.arange(length)
    table = np.zeros((length, length))
    for j in range(half):
        turn = 2 * np.pi * ((j * steps) % length) / length
        table[j] = np.cos(turn)
        table[half + j] = -np.sin(turn)
    table[half] = np.cos(2 * np.pi * ((half * steps) % length) / length)
    return table * growth_of(length)[None, :]


def inverse_matrix(length):
    half = length // 2
    steps = np.arange(length)
    table = np.zeros((length, length))
    for j in range(half):
        turn = 2 * np.pi * ((j * steps) % length) / length
        weight = 1.0 if j == 0 else 2.0
        table[:, j] = weight * np.cos(turn) / length
        table[:, half + j] = -weight * np.sin(turn) / length
    table[:, half] = np.cos(2 * np.pi * ((half * steps) % length) / length) / length
    return table / growth_of(length)[:, None]


def block_forward(length, rows):
    full = np.einsum("cn,rs->rcns", forward_matrix(length), np.eye(rows))
    return full.reshape(rows * length, length * rows).astype(np.float32)


def block_inverse(length, rows):
    full = np.einsum("nc,rs->nrsc", inverse_matrix(length), np.eye(rows))
    return full.reshape(length * rows, rows * length).astype(np.float32)


def channel_shifts(length):
    half = length // 2
    root = math.exp(math.log(circulant_alpha) / length)
    freq = np.concatenate([np.arange(half), np.arange(half)])
    freq[half] = half
    angle = 2 * np.pi * freq / length
    real = 1 - root * np.cos(angle)
    imag = root * np.sin(angle)
    imag[0] = 0.0
    imag[half] = 0.0
    return real, imag


def power_table(length):
    real, imag = channel_shifts(length)
    base = np.stack([real**2 + imag**2, 2 * real, np.ones_like(real)], axis=1)
    powers = [np.concatenate([np.ones((length, 1)), np.zeros((length, MOMENTS - 1))], axis=1)]
    for _ in range(DEPTH):
        last = powers[-1]
        following = np.zeros_like(last)
        for m in range(3):
            following[:, m:] += base[:, m : m + 1] * last[:, : MOMENTS - m]
        powers.append(following)
    return np.stack(powers)


def face_weights(padded_rows):
    centre = padded_rows[1:-1]
    columns = jnp.pad(centre, ((0, 0), (1, 1)), mode="edge")
    return (
        0.5 * (centre + padded_rows[:-2]),
        0.5 * (centre + padded_rows[2:]),
        0.5 * (centre + columns[:, :-2]),
        0.5 * (centre + columns[:, 2:]),
    )


def apply_faces(padded_rows, weights):
    north, south, west, east = weights
    centre = padded_rows[..., 1:-1, :]
    columns = jnp.pad(centre, [(0, 0)] * (centre.ndim - 1) + [(1, 1)])
    return (
        (north + south + west + east) * centre
        - north * padded_rows[..., :-2, :]
        - south * padded_rows[..., 2:, :]
        - west * columns[..., :-2]
        - east * columns[..., 2:]
    )


def borders_body(iterate_ref, forcing_ref, diff_ref, mine_ref, last_ref, rim_ref, done):
    steps, rows_dev, _ = iterate_ref.shape
    start = pl.multiple_of(jnp.where(lax.axis_index("rows") == 0, rows_dev - PAD, 0), 8)
    copies = []
    for s in range(steps):
        copies.append((iterate_ref.at[s, pl.ds(start, PAD)], mine_ref.at[pl.ds(PAD * s, PAD)]))
        at = PAD * (steps + s)
        copies.append((forcing_ref.at[s, pl.ds(start, PAD)], mine_ref.at[pl.ds(at, PAD)]))
    copies.append((diff_ref.at[pl.ds(start, PAD)], mine_ref.at[pl.ds(2 * PAD * steps, PAD)]))
    copies.append((diff_ref.at[pl.ds(0, PAD)], rim_ref.at[pl.ds(0, PAD)]))
    copies.append((diff_ref.at[pl.ds(rows_dev - PAD, PAD)], rim_ref.at[pl.ds(PAD, PAD)]))
    copies.append((iterate_ref.at[steps - 1], last_ref))
    started = []
    for index, (source, target) in enumerate(copies):
        started.append(pltpu.make_async_copy(source, target, done.at[index]))
        started[-1].start()
    for copy in started:
        copy.wait()


def pack(out_ref, at, source_ref, slab, halo, flip=0):
    rows = slab + 2 * halo
    for target in range(out_ref.shape[0]):
        first = slab * target + PAD - halo
        for t in range(source_ref.shape[-1] // 128):
            out_ref[target ^ flip, at + rows * t : at + rows * (t + 1), :] = source_ref[
                first : first + rows, 128 * t : 128 * (t + 1)
            ]


def later_steps_body(slab, halo, wide_ref, pieces_ref):
    steps, _, columns = wide_ref.shape
    for s in range(1, steps):
        at = (s - 1) * (columns // 128) * (slab + 2 * halo)
        pack(pieces_ref, at, wide_ref.at[s], slab, halo)


def first_step_body(slab, halo, rank_ref, partial_ref, previous_ref, low_ref, high_ref,
                    pieces_ref, squares_ref, whole_ref):
    rows_dev, columns = previous_ref.shape
    keep_low = jnp.where(rank_ref[0] == 0, 0.0, 1.0)
    keep_high = jnp.where(rank_ref[0] == rank_ref[1] - 1, 0.0, 1.0)
    whole_ref[:PAD, :] = partial_ref[0, :PAD, :] + keep_low * low_ref[...]
    whole_ref[PAD + rows_dev :, :] = partial_ref[0, PAD + rows_dev :, :] + keep_high * high_ref[...]
    squares = jnp.zeros((8, columns), jnp.float32)
    for at in range(0, rows_dev, 8):
        value = partial_ref[0, PAD + at : PAD + at + 8, :] + previous_ref[at : at + 8, :]
        whole_ref[PAD + at : PAD + at + 8, :] = value
        squares = squares + value * value
    total = squares[:, :128]
    for t in range(1, columns // 128):
        total = total + squares[:, 128 * t : 128 * t + 128]
    squares_ref[0] = total
    pack(pieces_ref, 0, whole_ref, slab, halo, rank_ref[2])


def put_weights(diff_ref, south_ref, east_ref, west_ref):
    rows, columns = diff_ref.shape
    centre = diff_ref[...]
    below = jnp.concatenate([centre[1:], centre[-1:]], axis=0)
    lane = lax.broadcasted_iota(jnp.int32, (rows, columns), 1)
    after = jnp.where(lane == columns - 1, centre, pltpu.roll(centre, columns - 1, 1))
    quarter = 0.5 * time_step
    south = quarter * (centre + below)
    east = quarter * (centre + after)
    west = (2.0 * quarter) * centre[:, :128]
    for r in range(rows):
        south_ref[8 * r : 8 * r + 8, :] = jnp.broadcast_to(south[r : r + 1], (8, columns))
        east_ref[8 * r : 8 * r + 8, :] = jnp.broadcast_to(east[r : r + 1], (8, columns))
        west_ref[8 * r : 8 * r + 8, :] = jnp.broadcast_to(west[r : r + 1], (8, 128))


def transform(target, early_ref, late_ref, mix, rows, length, tiles):
    sources = early_ref.shape[0]
    steps_dev = length // sources
    starts = list(range(0, rows - 7, 8))
    if starts[-1] + 8 < rows:
        starts.append(rows - 8)
    for start in starts:
        for t in range(tiles):
            cells = []
            for source in range(sources):
                for step in range(steps_dev):
                    ref = late_ref if step == 0 else early_ref
                    at = (max(step - 1, 0) * tiles + t) * rows + start
                    cells.append(ref[source, at : at + 8, :])
            target[start * length : (start + 8) * length, 128 * t : 128 * t + 128] = jnp.dot(
                mix,
                jnp.concatenate(cells, axis=0),
                precision=lax.Precision.HIGH,
                preferred_element_type=jnp.float32,
            )


def krylov_body(length, slab, halo, sources, place_ref, early_ref, diff_ref, mix_ref, *rest):
    pieces = rest[:sources]
    vectors = rest[sources : sources + DEPTH]
    moments_ref, late_ref, south_ref, east_ref, west_ref = rest[sources + DEPTH :]
    rows = slab + 2 * halo
    columns = diff_ref.shape[-1]
    groups = length // 8
    tiles = columns // 128
    first_row = place_ref[0] + halo == 0
    last_row = place_ref[0] + halo + slab == place_ref[1]
    keep_above = jnp.where(first_row, 0.0, 1.0)
    keep_below = jnp.where(last_row, 0.0, 1.0)
    put_weights(diff_ref, south_ref, east_ref, west_ref)
    for index, piece in enumerate(pieces):
        late_ref[index ^ place_ref[2]] = piece[...]
    transform(vectors[0], early_ref, late_ref, mix_ref[...], rows, length, tiles)

    lane8 = lax.broadcasted_iota(jnp.int32, (8, 128), 1)
    is_first = lane8 == 0
    is_last = lane8 == 127

    def load(source, r, group):
        at = pl.multiple_of(r * length + 8 * group, 8)
        return [source[pl.ds(at, 8), 128 * t : 128 * t + 128] for t in range(tiles)]

    def row_of(ref, r, t):
        return ref[pl.ds(pl.multiple_of(8 * r, 8), 8), 128 * t : 128 * t + 128]

    def south_flux(r, here, under):
        return [row_of(south_ref, r, t) * (under[t] - here[t]) for t in range(tiles)]

    def stencil(r, here, under, north):
        south = south_flux(r, here, under)
        turned = [pltpu.roll(v, 127, 1) for v in here] + [0.0]
        east = [
            row_of(east_ref, r, t) * (jnp.where(is_last, turned[t + 1], turned[t]) - here[t])
            for t in range(tiles)
        ]
        moved = [row_of(west_ref, r, 0) * here[0]] + [pltpu.roll(f, 1, 1) for f in east]
        value = [
            (jnp.where(is_first, moved[t], moved[t + 1]) - east[t]) + (north[t] - south[t])
            for t in range(tiles)
        ]
        return value, south

    def total(parts):
        while len(parts) > 1:
            parts = [parts[i] + parts[i + 1] for i in range(0, len(parts) - 1, 2)] + (
                [parts[-1]] if len(parts) % 2 else []
            )
        return parts[0]

    table = [jnp.zeros((8, 128), jnp.float32) for _ in range(groups)]

    def put(entry, index, sums):
        return jnp.where(lane8 == index, jnp.sum(sums, axis=1, keepdims=True), entry)

    for power in range(DEPTH):
        source = vectors[power]
        target = vectors[power + 1] if power + 1 < DEPTH else None
        first, final = power + 1, rows - 1 - power
        for group in range(groups):

            def step(r, carry, summing):
                here, north, sums = carry
                under = load(source, r + 1, group)
                value, south = stencil(r, here, under, north)
                if target is not None:
                    at = pl.multiple_of(r * length + 8 * group, 8)
                    for t in range(tiles):
                        target[pl.ds(at, 8), 128 * t : 128 * t + 128] = value[t]
                if summing:
                    products = [
                        sums[0] + total([v * v for v in here]),
                        sums[1] + total([v * w for v, w in zip(here, value)]),
                    ]
                    if target is None:
                        products.append(sums[2] + total([w * w for w in value]))
                    sums = tuple(products)
                return tuple(under), tuple(south), sums

            top = load(source, first - 1, group)
            here = load(source, first, group)
            carry = (tuple(here), tuple(south_flux(first - 1, top, here)), ())
            if first < halo:
                carry = lax.fori_loop(
                    first, halo, functools.partial(step, summing=False), carry, unroll=True
                )
            zero = jnp.zeros((8, 128), jnp.float32)
            carry = (carry[0], carry[1], (zero,) * (2 if target is not None else 3))
            carry = lax.fori_loop(
                halo, halo + slab, functools.partial(step, summing=True), carry, unroll=min(UNROLL, max(1, slab // 2))
            )
            for index, sums in enumerate(carry[2]):
                table[group] = put(table[group], 2 * power + index, sums)
            if first < halo:
                carry = (carry[0], carry[1], ())
                lax.fori_loop(
                    halo + slab, final, functools.partial(step, summing=False), carry, unroll=True
                )
            if target is not None and first < halo:
                for r, keep in ((halo - 1, keep_above), (halo + slab, keep_below)):
                    at = r * length + 8 * group
                    target[at : at + 8, :] = target[at : at + 8, :] * keep
    moments_ref[...] = jnp.concatenate(table, axis=0)


def combine_body(length, slab, halo, moments_ref, table_ref, shift_ref, mix_ref, *rest):
    power_refs = rest[:DEPTH]
    out_ref, doubt_ref = rest[DEPTH:]
    steps_dev = out_ref.shape[1] // slab
    half = length // 2
    own = moments_ref[...]
    swapped = jnp.concatenate([own[half:], own[:half]], axis=0)
    channel = lax.broadcasted_iota(jnp.int32, own.shape, 0)
    alone = (channel == 0) | (channel == half)
    sums = jnp.where(alone, own, own + swapped)
    mu = [
        jnp.sum(sums * table_ref[k + 1], axis=1, keepdims=True) for k in range(2 * CG_ITERS)
    ]
    low1, low2 = mu[2] / mu[1], mu[3] / mu[1]
    pivot1 = mu[3] - low1 * mu[2]
    cross = mu[4] - low1 * mu[3]
    pivot2 = mu[5] - low2 * mu[3]
    right1 = mu[1] - low1 * mu[0]
    right2 = mu[2] - low2 * mu[0]
    low3 = cross / pivot1
    pivot2 = pivot2 - low3 * cross
    right2 = right2 - low3 * right1
    sound = (pivot1 > LEAST_PIVOTS[0] * mu[3]) & (pivot2 > LEAST_PIVOTS[1] * mu[5])
    doubt = jnp.max(jnp.where(sound, 0.0, 1.0), axis=0, keepdims=True)
    doubt_ref[...] = jnp.broadcast_to(doubt, doubt_ref.shape)
    c2 = right2 / pivot2
    c1 = (right1 - cross * c2) / pivot1
    c0 = (mu[0] - mu[2] * c1 - mu[3] * c2) / mu[1]
    inner = c0 * table_ref[0] + c1 * table_ref[1] + c2 * table_ref[2]
    real = shift_ref[0]
    imag = shift_ref[1]
    lanes = lax.broadcasted_iota(jnp.int32, inner.shape, 1)
    outer = real * inner + jnp.where(lanes == 0, 0.0, pltpu.roll(inner, 1, 1))
    crossed = imag * inner
    sign = jnp.where(lax.broadcasted_iota(jnp.int32, inner.shape, 0) < half, 1.0, -1.0)
    crossed = sign * crossed
    columns = out_ref.shape[-1]

    def spread(values, index):
        return jnp.broadcast_to(values[:, index : index + 1], (length, columns))[None]

    for start in range(0, slab, 8):
        total = jnp.zeros((8, length, columns), jnp.float32)
        other = jnp.zeros((8, length, columns), jnp.float32)
        for power in range(DEPTH):
            at = (halo + start) * length
            here = power_refs[power][at : at + 8 * length, :].reshape(8, length, columns)
            total = total + spread(outer, power) * here
            if power + 1 < DEPTH:
                flipped = jnp.concatenate([here[:, half:], here[:, :half]], axis=1)
                other = other + spread(crossed, power) * flipped
        block = (total + other).reshape(8 * length, columns)
        result = jnp.dot(
            mix_ref[...], block, precision=lax.Precision.HIGHEST, preferred_element_type=jnp.float32
        )
        for step in range(length):
            at = (step % steps_dev) * slab + start
            out_ref[step // steps_dev, at : at + 8, :] = result[step * 8 : step * 8 + 8]


def iteration(iterate, forcing, initial_state, diffusivity):
    steps_dev, rows_dev, columns_dev = iterate.shape
    time_devices = lax.axis_size("tm")
    row_devices = lax.axis_size("rows")
    time_rank = lax.axis_index("tm")
    row_rank = lax.axis_index("rows")
    length = steps_dev * time_devices
    cell_count = rows_dev * row_devices * columns_dev
    slab = rows_dev // time_devices
    halo = DEPTH
    rows = slab + 2 * halo

    tiles = columns_dev // 128
    vmem = pl.BlockSpec(memory_space=pltpu.VMEM)
    smem = pl.BlockSpec(memory_space=pltpu.SMEM)
    params = pltpu.CompilerParams(vmem_limit_bytes=24 * 2**20)
    rank = jnp.stack([row_rank, jnp.int32(row_devices), time_rank]).astype(jnp.int32)

    if row_devices == 2:
        mine, last, rim = pl.pallas_call(
            borders_body,
            out_shape=[
                pltpu.VMEM(((2 * steps_dev + 1) * PAD, columns_dev), jnp.float32),
                pltpu.VMEM((rows_dev, columns_dev), jnp.float32),
                pltpu.VMEM((2 * PAD, columns_dev), jnp.float32),
            ],
            in_specs=[pl.BlockSpec(memory_space=pltpu.HBM)] * 3,
            out_specs=[vmem] * 3,
            scratch_shapes=[pltpu.SemaphoreType.DMA((2 * steps_dev + 4,))],
            compiler_params=pltpu.CompilerParams(vmem_limit_bytes=2**26 - 3 * 2**18),
            name="borders",
        )(iterate, forcing, diffusivity)
        low = high = lax.ppermute(mine, "rows", [(0, 1), (1, 0)])
    else:
        last = iterate[-1]
        rim = jnp.concatenate([diffusivity[:PAD], diffusivity[-PAD:]])
        low, high = border_rows((iterate, forcing, diffusivity), "rows", PAD)
    arriving = from_behind(last, "tm", 1)

    keep_low = jnp.where(row_rank == 0, 0.0, 1.0)
    keep_high = jnp.where(row_rank == row_devices - 1, 0.0, 1.0)

    def widened(block, slot):
        shape = (steps_dev, PAD, columns_dev)
        at = slice(slot * PAD, (slot + steps_dev) * PAD)
        return jnp.concatenate(
            [keep_low * low[at].reshape(shape), block, keep_high * high[at].reshape(shape)], axis=1
        )

    diff_low = jnp.where(row_rank == 0, rim[:1], low[-PAD:])
    diff_high = jnp.where(row_rank == row_devices - 1, rim[-1:], high[-PAD:])
    rimmed = jnp.concatenate([diff_low, diffusivity, diff_high])
    wide_iterate = widened(iterate, 0)
    faces = face_weights(jnp.pad(rimmed, ((1, 1), (0, 0)), mode="edge"))
    wide_rows = jnp.pad(wide_iterate, ((0, 0), (1, 1), (0, 0)))
    wide = time_step * (widened(forcing, steps_dev) - apply_faces(wide_rows, faces)) - wide_iterate
    wide = wide + jnp.concatenate([jnp.zeros_like(wide_iterate[:1]), wide_iterate[:-1]])
    at_row = lax.broadcasted_iota(jnp.int32, (1, rows_dev + 2 * PAD, 1), 1)
    keep = jnp.where(at_row < PAD, keep_low, jnp.where(at_row < PAD + rows_dev, 1.0, keep_high))
    wide = wide * keep
    own = wide[1:, PAD : PAD + rows_dev]
    squares_late = jnp.sum(own * own, axis=(1, 2))

    padded = rows_dev + 2 * PAD
    early = pl.pallas_call(
        functools.partial(later_steps_body, slab, halo),
        out_shape=jax.ShapeDtypeStruct(
            (time_devices, (steps_dev - 1) * tiles * rows, 128), jnp.float32
        ),
        in_specs=[vmem],
        out_specs=vmem,
        compiler_params=params,
        name="later_steps",
    )(wide)
    early = lax.all_to_all(early, "tm", split_axis=0, concat_axis=0, tiled=True)

    previous = jnp.where(time_rank == 0, initial_state, arriving)
    before_low, before_high = border_rows((previous,), "rows", PAD)
    late, squares_first = pl.pallas_call(
        functools.partial(first_step_body, slab, halo),
        out_shape=[
            jax.ShapeDtypeStruct((time_devices, tiles * rows, 128), jnp.float32),
            jax.ShapeDtypeStruct((1, 8, 128), jnp.float32),
        ],
        in_specs=[smem] + [vmem] * 4,
        out_specs=[vmem] * 2,
        scratch_shapes=[pltpu.VMEM((padded, columns_dev), jnp.float32)],
        compiler_params=params,
        name="first_step",
    )(rank, wide, previous, before_low, before_high)
    late = exchanged(late)

    squares = jnp.concatenate([jnp.sum(squares_first, axis=(1, 2)), squares_late])
    residual_rms = jnp.sqrt(lax.psum(squares, "rows") / cell_count + rms_eps)

    diff_slab = lax.dynamic_slice_in_dim(rimmed, slab * time_rank + PAD - halo, rows, axis=0)
    place = jnp.stack(
        [
            row_rank * rows_dev + time_rank * slab - halo,
            jnp.int32(rows_dev * row_devices),
            time_rank,
        ]
    ).astype(jnp.int32)

    vector = pltpu.VMEM((rows * length, columns_dev), jnp.float32)
    *powers, moments = pl.pallas_call(
        functools.partial(krylov_body, length, slab, halo, time_devices),
        out_shape=[vector] * DEPTH + [jax.ShapeDtypeStruct((length, 128), jnp.float32)],
        in_specs=[smem] + [vmem] * (3 + time_devices),
        out_specs=[vmem] * (DEPTH + 1),
        scratch_shapes=[
            pltpu.VMEM((time_devices, tiles * rows, 128), jnp.float32),
            pltpu.VMEM((rows * 8, columns_dev), jnp.float32),
            pltpu.VMEM((rows * 8, columns_dev), jnp.float32),
            pltpu.VMEM((rows * 8, 128), jnp.float32),
        ],
        compiler_params=pltpu.CompilerParams(vmem_limit_bytes=24 * 2**20),
        name="krylov",
    )(place, early, diff_slab, jnp.asarray(block_forward(length, 8)), *late)

    moments = summed_over_group(moments)

    real, imag = channel_shifts(length)
    shift = np.broadcast_to(np.stack([real, imag])[:, :, None], (2, length, 128))
    table = np.zeros((DEPTH + 1, length, 128))
    table[:, :, :MOMENTS] = power_table(length)
    corrected, doubt = pl.pallas_call(
        functools.partial(combine_body, length, slab, halo),
        out_shape=[
            jax.ShapeDtypeStruct((time_devices, steps_dev * slab, columns_dev), jnp.float32),
            jax.ShapeDtypeStruct((8, 128), jnp.float32),
        ],
        in_specs=[vmem] * (4 + DEPTH),
        out_specs=[vmem] * 2,
        compiler_params=params,
        name="combine",
    )(
        moments,
        jnp.asarray(table, jnp.float32),
        jnp.asarray(shift, jnp.float32),
        jnp.asarray(block_inverse(length, 8)),
        *powers,
    )
    back = lax.all_to_all(corrected, "tm", split_axis=0, concat_axis=0, tiled=True)

    def redone(trip, _):
        inputs = (iterate, forcing, initial_state, diffusivity)
        return careful_correction(*[jnp.where(trip < 2, value, 0.0) for value in inputs])

    back = lax.fori_loop(0, doubt[0, 0].astype(jnp.int32), redone, back)
    updated = pl.pallas_call(
        functools.partial(finish_body, slab),
        out_shape=jax.ShapeDtypeStruct(iterate.shape, jnp.float32),
        in_specs=[vmem, pl.BlockSpec(memory_space=pl.ANY)],
        out_specs=pl.BlockSpec(memory_space=pltpu.HBM),
        scratch_shapes=[
            pltpu.VMEM(back.shape, jnp.float32),
            pltpu.VMEM(iterate.shape, jnp.float32),
            pltpu.SemaphoreType.DMA((time_devices,)),
            pltpu.SemaphoreType.DMA((time_devices,)),
        ],
        compiler_params=params,
        name="finish",
    )(iterate, back)
    return (updated, residual_rms)


def solution(mesh):
    placed = (
        P(("groups", "tm"), "rows", None),
        P(("groups", "tm"), "rows", None),
        P(("groups", "rows"), None),
        P(("groups", "rows"), None),
    )
    return jax.shard_map(
        iteration,
        mesh=mesh,
        in_specs=placed,
        out_specs=(P(("groups", "tm"), "rows", None), P(("groups", "tm"))),
        check_vma=False,
    )
```
